128 devices in a mesh: lat: 8 (over z_lo, x), lon: 16 (over y, z_hi, core).
Axes of the slice: x: 4, y: 4, z: 4 (z_hi: 2, z_lo: 2; z = z_hi * 2 + z_lo), core: 2. Of those that a mesh axis runs over, the one named last changes fastest.
Arguments:
- input_field: bfloat16 [1024, 1024, 128], P('lat', 'lon'), may hold values from -6 to 6
- conv_one: bfloat16 [3, 3, 128, 128], replicated, may hold values from -0.1875 to 0.1875
- conv_two: bfloat16 [3, 3, 128, 128], replicated, may hold values from -0.1875 to 0.1875
- merge_weight: bfloat16 [512, 512], replicated, may hold values from -0.25 to 0.25
- norm_gains: float32 [4, 512], replicated, may hold values from 0.1 to 1.9
- attention_in: bfloat16 [512, 1536], replicated, may hold values from -0.25 to 0.25
- attention_out: bfloat16 [512, 512], replicated, may hold values from -0.25 to 0.25
- dense_in: bfloat16 [512, 2048], replicated, may hold values from -0.25 to 0.25
- dense_out: bfloat16 [2048, 512], replicated, may hold values from -0.125 to 0.125
- expand_weight: bfloat16 [512, 512], replicated, may hold values from -0.25 to 0.25
Outputs:
- output_field: bfloat16 [1024, 1024, 128], P('lat', 'lon')
The draws below stay inside these ranges and needn't reach their ends.
All inputs are finite; a program needn't handle non-finite values.
Results may differ from the reference program's by a relative error of at most 0.0095.
Values may be sent and summed in bfloat16 or wider, within the bound.
No kernel may reach another device: no remote copies, remote signals or barrier semaphores. Data moves between devices by JAX's collectives and lax.ppermute only.
A program may use at most 128 MiB of HBM per device.

```python
import jax
import jax.numpy as jnp
from jax import lax

CHANNELS = 128
LATENT = 512
NUM_HEADS = 16
MLP_WIDTH = 2048
WINDOW = 16
HEAD_WIDTH = 32
LAT_CELLS = 1024
LON_CELLS = 1024


def level_of(stream_key, dims, shards, smallest, largest):
    factor_of = 1.0
    for axis_at, blocks in shards:
        draws = jax.random.uniform(jax.random.fold_in(jax.random.fold_in(stream_key, 6), axis_at), (blocks,), jnp.float32, smallest / len(shards), largest / len(shards))
        factor_of = factor_of * jnp.repeat(jnp.exp(draws), dims[axis_at] // blocks).reshape((-1,) + (1,) * (len(dims) - 1 - axis_at))
    return factor_of


def gaussian(own_key, extent, scale, bound, shards=(), kind=jnp.bfloat16):
    entries = scale * jax.random.normal(own_key, extent, jnp.float32)
    if shards:
        entries = entries * level_of(own_key, extent, shards, -0.22, 0.18)
    return jnp.clip(entries, -bound, bound).astype(kind)


def setup_inputs(seed: int = 0) -> dict:
    keys = jax.random.split(jax.random.key(seed), 11)
    return {
        "input_field": gaussian(keys[0], (LAT_CELLS, LON_CELLS, CHANNELS), 1.0, 6.0, ((0, 8), (1, 16))),
        "conv_one": gaussian(keys[1], (3, 3, CHANNELS, CHANNELS), (9 * CHANNELS) ** -0.5, 0.1875),
        "conv_two": gaussian(keys[2], (3, 3, CHANNELS, CHANNELS), (9 * CHANNELS) ** -0.5, 0.1875),
        "merge_weight": gaussian(keys[3], (4 * CHANNELS, LATENT), (4 * CHANNELS) ** -0.5, 0.25),
        "norm_gains": jnp.clip(1.0 + 0.18 * jax.random.normal(keys[4], (4, LATENT), jnp.float32), 0.1, 1.9),
        "attention_in": gaussian(keys[5], (LATENT, 3 * LATENT), LATENT ** -0.5, 0.25),
        "attention_out": gaussian(keys[6], (LATENT, LATENT), LATENT ** -0.5, 0.25),
        "dense_in": gaussian(keys[7], (LATENT, MLP_WIDTH), LATENT ** -0.5, 0.25),
        "dense_out": gaussian(keys[8], (MLP_WIDTH, LATENT), MLP_WIDTH ** -0.5, 0.125),
        "expand_weight": gaussian(keys[9], (LATENT, 4 * CHANNELS), LATENT ** -0.5, 0.25),
    }


EPSILON = 1e-06
FLOOR = 0.75

def conv_gelu(source, kernel, padding):
    result = lax.conv_general_dilated(source[None], kernel, (1, 1), padding, dimension_numbers=('NHWC', 'HWIO', 'NHWC'), preferred_element_type=jnp.float32)[0]
    return jax.nn.gelu(result)

def layer_norm(stream, gain):
    center = stream - lax.optimization_barrier(jnp.mean(stream, axis=-1, keepdims=True))
    spread = lax.optimization_barrier(jnp.mean(center * center, axis=-1, keepdims=True))
    return center * lax.rsqrt(spread + EPSILON) * gain

def head_norm(stream, gain):
    square = lax.optimization_barrier(jnp.mean(stream * stream, axis=-1, keepdims=True))
    return stream * gain / jnp.sqrt(jnp.maximum(square, FLOOR))

def project_heads(tokens, norm_gains, attention_in):
    count = tokens.shape[0]
    normed = layer_norm(tokens.astype(jnp.float32), norm_gains[0]).astype(jnp.bfloat16)
    projected = jnp.dot(normed, attention_in, preferred_element_type=jnp.float32)
    split_shape = (count, NUM_HEADS, HEAD_WIDTH)
    queries = head_norm(projected[:, :LATENT].reshape(split_shape), norm_gains[1].reshape(NUM_HEADS, HEAD_WIDTH)).astype(jnp.bfloat16)
    key_rows = head_norm(projected[:, LATENT:2 * LATENT].reshape(split_shape), norm_gains[2].reshape(NUM_HEADS, HEAD_WIDTH)).astype(jnp.bfloat16)
    values = projected[:, 2 * LATENT:].reshape(split_shape).astype(jnp.bfloat16)
    return (queries, key_rows, values)

def attend_window(queries, key_rows, values):
    scores = jnp.einsum('qhd,khd->hqk', queries.astype(jnp.float32), key_rows.astype(jnp.float32)) * HEAD_WIDTH ** (-0.5)
    expon = jnp.exp(scores)
    weights = (expon / lax.optimization_barrier(jnp.sum(expon, axis=-1, keepdims=True))).astype(jnp.bfloat16)
    gathered = jnp.einsum('hqk,khd->qhd', weights.astype(jnp.float32), values.astype(jnp.float32))
    return gathered.reshape(queries.shape[0], LATENT).astype(jnp.bfloat16)

def finish(tokens, attended, norm_gains, attention_out, dense_in, dense_out):
    mixed_tokens = (tokens.astype(jnp.float32) + jnp.dot(attended, attention_out, preferred_element_type=jnp.float32)).astype(jnp.bfloat16)
    normed_two = layer_norm(mixed_tokens.astype(jnp.float32), norm_gains[3]).astype(jnp.bfloat16)
    inner_units = jax.nn.gelu(jnp.dot(normed_two, dense_in, preferred_element_type=jnp.float32)).astype(jnp.bfloat16)
    return (mixed_tokens.astype(jnp.float32) + jnp.dot(inner_units, dense_out, preferred_element_type=jnp.float32)).astype(jnp.bfloat16)

def reference(input_field, conv_one, conv_two, merge_weight, norm_gains, attention_in, attention_out, dense_in, dense_out, expand_weight):
    first = conv_gelu(input_field, conv_one, 'SAME').astype(jnp.bfloat16)
    second = conv_gelu(first, conv_two, 'SAME').astype(jnp.bfloat16)
    half_lat = LAT_CELLS // 2
    half_lon = LON_CELLS // 2
    offset_lat = half_lat // WINDOW
    offset_lon = half_lon // WINDOW
    patches = second.reshape(half_lat, 2, half_lon, 2, CHANNELS).transpose(0, 2, 1, 3, 4).reshape(half_lat * half_lon, 4 * CHANNELS)
    coarse = jnp.dot(patches, merge_weight, preferred_element_type=jnp.float32).astype(jnp.bfloat16)
    grouped = coarse.reshape(WINDOW, offset_lat, WINDOW, offset_lon, LATENT).transpose(1, 3, 0, 2, 4).reshape(offset_lat * offset_lon, WINDOW * WINDOW, LATENT)

    def one_window(tokens):
        queries, key_rows, values = project_heads(tokens, norm_gains, attention_in)
        attended = attend_window(queries, key_rows, values)
        return finish(tokens, attended, norm_gains, attention_out, dense_in, dense_out)
    updated = lax.map(one_window, grouped)
    placed = updated.reshape(offset_lat, offset_lon, WINDOW, WINDOW, LATENT).transpose(2, 0, 3, 1, 4).reshape(half_lat * half_lon, LATENT)
    expanded = jnp.dot(placed, expand_weight, preferred_element_type=jnp.float32)
    expanded = expanded.reshape(half_lat, half_lon, 2, 2, CHANNELS).transpose(0, 2, 1, 3, 4).reshape(LAT_CELLS, LON_CELLS, CHANNELS)
    return (expanded + input_field.astype(jnp.float32)).astype(jnp.bfloat16)
```

```python
import functools
import math

import jax
import jax.numpy as jnp
from jax import lax
from jax.experimental import pallas as pl
from jax.experimental.pallas import tpu as pltpu
from jax.sharding import PartitionSpec as P

CHANNELS = 128
LATENT = 512
NUM_HEADS = 16
HEAD_WIDTH = 32
MLP_WIDTH = 2048
EPSILON = 1e-06
FLOOR = 0.75
GELU_ONE = math.sqrt(2.0 / math.pi)
GELU_TWO = GELU_ONE * 0.044715

ROWS, COLS = 128, 64
PAIRS = COLS // 2
STRIDE = 80
LEAD = 8
STAGE_ROWS = 28
FIRST_ROWS = 24
FIRST_STRIDE = 40
INNER, OUTER = (1, 2), (0, 3)
WINDOWS = 4
MIB = 1 << 20


def gelu(v):
    half = 0.5 * v
    return half + half * jnp.tanh(v * (GELU_ONE + GELU_TWO * (v * v)))


def front_kernel(blocks, keep_ref, x_ref, left_ref, right_ref, *rest):
    if blocks == OUTER:
        top_ref, bottom_ref = rest[:2]
        rest = rest[2:]
    w1_ref, w2_ref, wm_ref, out_ref, stage, sides, xab, firsts, fab = rest
    sides[0:2] = left_ref[...].astype(jnp.float32)
    sides[2:4] = right_ref[...].astype(jnp.float32)
    sub = lax.broadcasted_iota(jnp.int32, (16, 8, LATENT), 1)
    for at, block in enumerate(blocks):
        for p in range(2):
            start = 64 * p + 16 * block - 2
            low, high = max(start, 0), min(start + 20, ROWS)
            skip, count = low - start, min(start + 20, ROWS) - low

            def place(r, carry, p=p, low=low, skip=skip):
                to = pl.multiple_of((p * STAGE_ROWS + skip + r) * STRIDE + LEAD, 8)
                stage[pl.ds(to, COLS), :] = x_ref[low + r].astype(jnp.float32)
                return carry

            lax.fori_loop(0, count, place, 0, unroll=2)
            base = (p * STAGE_ROWS + skip) * STRIDE
            for c in range(2):
                stage[pl.ds(base + LEAD - 2 + c, count, stride=STRIDE), :] = sides[c, low:high, :]
                stage[pl.ds(base + LEAD + COLS + c, count, stride=STRIDE), :] = sides[
                    2 + c, low:high, :
                ]
            if skip > 0:
                for r in range(2):
                    to = (p * STAGE_ROWS + r) * STRIDE
                    stage[to : to + STRIDE, :] = top_ref[r].astype(jnp.float32)
            if skip + count < 20:
                for r in range(2):
                    to = (p * STAGE_ROWS + 18 + r) * STRIDE
                    stage[to : to + STRIDE, :] = bottom_ref[r].astype(jnp.float32)
        for p in range(2):
            for r in range(20):
                base = (p * STAGE_ROWS + r) * STRIDE + LEAD
                xab[p, r] = jnp.concatenate(
                    [stage[pl.ds(base + k, PAIRS, stride=2), :] for k in (-2, -1, 0, 1)], axis=-1
                ).astype(jnp.bfloat16)
        for p in range(2):
            for r0 in (0, 9):
                lhs = jnp.concatenate([xab[p, r0 + dy : r0 + dy + 9] for dy in range(3)], axis=-1)
                y = gelu(
                    jnp.dot(
                        lhs.reshape(9 * PAIRS, 1536),
                        w1_ref[...],
                        preferred_element_type=jnp.float32,
                    )
                )
                for r in range(9):
                    to = (p * FIRST_ROWS + r0 + r) * FIRST_STRIDE
                    for m in range(2):
                        firsts[m, to : to + PAIRS, :] = y[
                            r * PAIRS : (r + 1) * PAIRS, m * CHANNELS : (m + 1) * CHANNELS
                        ]
        lhs = jnp.concatenate(
            [
                jnp.concatenate(
                    [
                        stage[
                            pl.ds(
                                (p * STAGE_ROWS + dy) * STRIDE + LEAD + COLS - 2 + k,
                                FIRST_ROWS,
                                stride=STRIDE,
                            ),
                            :,
                        ]
                        for dy in range(3)
                        for k in range(4)
                    ],
                    axis=-1,
                )
                for p in range(2)
            ],
            axis=0,
        ).astype(jnp.bfloat16)
        edge = gelu(jnp.dot(lhs, w1_ref[...], preferred_element_type=jnp.float32))
        for p in range(2):
            base = p * FIRST_ROWS * FIRST_STRIDE
            mine = edge[p * FIRST_ROWS : (p + 1) * FIRST_ROWS]
            last = pl.ds(base + PAIRS, FIRST_ROWS, stride=FIRST_STRIDE)
            firsts[0, last, :] = mine[:, 0:CHANNELS]
            firsts[1, last, :] = mine[:, CHANNELS:] * keep_ref[1]
            begin = pl.ds(base, FIRST_ROWS, stride=FIRST_STRIDE)
            firsts[0, begin, :] = firsts[0, begin, :] * keep_ref[0]
        if block == 0:
            firsts[:, 0:FIRST_STRIDE, :] = firsts[:, 0:FIRST_STRIDE, :] * keep_ref[2]
        if block == 3:
            to = (FIRST_ROWS + 17) * FIRST_STRIDE
            firsts[:, to : to + FIRST_STRIDE, :] = firsts[:, to : to + FIRST_STRIDE, :] * keep_ref[3]
        for p in range(2):
            for r in range(18):
                base = (p * FIRST_ROWS + r) * FIRST_STRIDE
                fab[p, r] = jnp.concatenate(
                    [firsts[m, base + k : base + k + PAIRS, :] for k in range(2) for m in range(2)],
                    axis=-1,
                ).astype(jnp.bfloat16)
        for j in range(2):
            coarse = []
            for p in range(2):
                lhs = jnp.concatenate(
                    [fab[p, 8 * j + dy : 8 * j + dy + 8] for dy in range(3)], axis=-1
                )
                s = gelu(
                    jnp.dot(
                        lhs.reshape(8 * PAIRS, 1536),
                        w2_ref[...],
                        preferred_element_type=jnp.float32,
                    )
                ).astype(jnp.bfloat16)
                s = s.reshape(4, 2, PAIRS, 256)
                patches = jnp.concatenate([s[:, 0], s[:, 1]], axis=-1).reshape(4 * PAIRS, LATENT)
                coarse.append(
                    jnp.dot(patches, wm_ref[...], preferred_element_type=jnp.float32).reshape(
                        16, 8, LATENT
                    )
                )
            zero, one = coarse
            even = jnp.where(sub < 4, zero, pltpu.roll(one, 4, 1))
            odd = jnp.where(sub < 4, pltpu.roll(zero, 4, 1), one)
            u0 = 8 * at + 4 * j
            out_ref[u0 : u0 + 4, :, 0] = even.reshape(4, 4, 8, LATENT).astype(jnp.bfloat16)
            out_ref[u0 : u0 + 4, :, 1] = odd.reshape(4, 4, 8, LATENT).astype(jnp.bfloat16)


def front(blocks, keep, x, left, right, ends, w1, w2, wm):
    vmem = pl.BlockSpec(memory_space=pltpu.VMEM)
    args = (x, left, right) + tuple(ends) + (w1, w2, wm)
    out = pl.pallas_call(
        functools.partial(front_kernel, blocks),
        out_shape=jax.ShapeDtypeStruct((16, 4, 2, 8, LATENT), jnp.bfloat16),
        in_specs=[pl.BlockSpec(memory_space=pltpu.SMEM)] + [vmem] * len(args),
        out_specs=vmem,
        scratch_shapes=[
            pltpu.VMEM((2 * STAGE_ROWS * STRIDE, CHANNELS), jnp.float32),
            pltpu.VMEM((4, ROWS, CHANNELS), jnp.float32),
            pltpu.VMEM((2, 20, PAIRS, 512), jnp.bfloat16),
            pltpu.VMEM((2, 2 * FIRST_ROWS * FIRST_STRIDE, CHANNELS), jnp.float32),
            pltpu.VMEM((2, 18, PAIRS, 512), jnp.bfloat16),
        ],
        compiler_params=pltpu.CompilerParams(vmem_limit_bytes=28 * MIB),
        cost_estimate=pl.CostEstimate(
            flops=8_000_000_000, transcendentals=1_100_000, bytes_accessed=5_000_000
        ),
        name="front_inner" if blocks == INNER else "front_outer",
    )(keep, *args)
    return out.reshape(128, 8, LATENT)


def layer_norm(v, gain):
    center = v - jnp.mean(v, axis=-1, keepdims=True)
    spread = jnp.mean(center * center, axis=-1, keepdims=True)
    return center * lax.rsqrt(spread + EPSILON) * gain


def middle_kernel(
    tok_ref, gains_ref, qgain_ref, win_ref, wout_ref, wi_ref, wd_ref, out_ref, cells
):
    step = pl.program_id(0)

    @pl.when(step == 0)
    def _():
        held = tok_ref[...].reshape(128 * 8, LATENT).astype(jnp.float32)
        for q in range(4):
            cells[q] = held[:, q * 128 : (q + 1) * 128]

    places = [pl.ds(step + WINDOWS * p, 128, stride=8) for p in range(2)]
    tokens = jnp.concatenate(
        [jnp.concatenate([cells[q, place, :] for q in range(4)], axis=-1) for place in places],
        axis=0,
    )
    normed = layer_norm(tokens, gains_ref[0:1, :]).astype(jnp.bfloat16)
    projected = lax.dot_general(
        win_ref[...], normed, (((1,), (1,)), ((), ())), preferred_element_type=jnp.float32
    )

    def scaled(part):
        heads = part.reshape(NUM_HEADS, HEAD_WIDTH, 256)
        square = jnp.mean(heads * heads, axis=1, keepdims=True)
        return (heads * lax.rsqrt(jnp.maximum(square, FLOOR))).reshape(LATENT, 256)

    qgain = jnp.concatenate([qgain_ref[...], qgain_ref[...]], axis=-1)
    queries = (scaled(projected[0:LATENT]) * qgain).astype(jnp.bfloat16)
    keys = scaled(projected[LATENT : 2 * LATENT]).T.astype(jnp.bfloat16)
    values = projected[2 * LATENT :].astype(jnp.bfloat16)
    ones = jnp.ones((16, 256), jnp.bfloat16)
    blank = jnp.zeros((HEAD_WIDTH, 256), jnp.bfloat16)
    attended = []
    for h in range(NUM_HEADS):
        rows = slice(h * HEAD_WIDTH, (h + 1) * HEAD_WIDTH)
        group = h // 4
        right = jnp.concatenate([queries[rows] if i == h % 4 else blank for i in range(4)], axis=0)
        scores = jnp.dot(
            keys[:, group * 128 : (group + 1) * 128], right, preferred_element_type=jnp.float32
        )
        expon = jnp.exp2(scores).astype(jnp.bfloat16)
        both = jnp.dot(
            jnp.concatenate([values[rows], ones], axis=0), expon, preferred_element_type=jnp.float32
        )
        attended.append(both[0:HEAD_WIDTH] / both[HEAD_WIDTH : HEAD_WIDTH + 1])
    attended = jnp.concatenate(attended, axis=0).T.astype(jnp.bfloat16)
    mixed = (
        tokens + jnp.dot(attended, wout_ref[...], preferred_element_type=jnp.float32)
    ).astype(jnp.bfloat16).astype(jnp.float32)
    normed_two = layer_norm(mixed, gains_ref[3:4, :]).astype(jnp.bfloat16)
    updated = mixed
    for j in range(4):
        part = slice(j * 512, (j + 1) * 512)
        inner = gelu(
            jnp.dot(normed_two, wi_ref[:, part], preferred_element_type=jnp.float32)
        ).astype(jnp.bfloat16)
        updated = updated + jnp.dot(inner, wd_ref[part, :], preferred_element_type=jnp.float32)
    for p in range(2):
        for q in range(4):
            cells[q, places[p], :] = updated[128 * p : 128 * (p + 1), 128 * q : 128 * (q + 1)]

    @pl.when(step == WINDOWS - 1)
    def _():
        held = jnp.concatenate([cells[q] for q in range(4)], axis=-1)
        out_ref[...] = held.astype(jnp.bfloat16).reshape(128, 8, LATENT)


def middle(tokens, gains, qgain, win, wout, wi, wd):
    whole = lambda *shape: pl.BlockSpec(
        shape, lambda i: (0,) * len(shape), pipeline_mode=pl.Buffered(1)
    )
    return pl.pallas_call(
        middle_kernel,
        out_shape=jax.ShapeDtypeStruct((128, 8, LATENT), jnp.bfloat16),
        grid=(WINDOWS,),
        in_specs=[
            whole(128, 8, LATENT),
            whole(4, LATENT),
            whole(LATENT, 128),
            whole(3 * LATENT, LATENT),
            whole(LATENT, LATENT),
            whole(LATENT, MLP_WIDTH),
            whole(MLP_WIDTH, LATENT),
        ],
        out_specs=pl.BlockSpec((128, 8, LATENT), lambda i: (0, 0, 0)),
        scratch_shapes=[pltpu.VMEM((4, 1024, 128), jnp.float32)],
        compiler_params=pltpu.CompilerParams(vmem_limit_bytes=32 * MIB),
        cost_estimate=pl.CostEstimate(
            flops=16_000_000_000, transcendentals=6_000_000, bytes_accessed=9_000_000
        ),
        name="middle",
    )(tokens, gains, qgain, win, wout, wi, wd)


def back_kernel(cells_ref, x_ref, we_ref, *rest):
    out_ref, even, odd = rest[-3:]
    expanded = jnp.dot(
        cells_ref[...].reshape(512, LATENT), we_ref[...], preferred_element_type=jnp.float32
    )
    for di, held in enumerate((even, odd)):
        for dj in range(2):
            lanes = (2 * di + dj) * CHANNELS
            held[pl.ds(dj, 512, stride=2), :] = expanded[:, lanes : lanes + CHANNELS]
    for di, held in enumerate((even, odd)):
        for u in range(8):
            rows = held[u * 128 : (u + 1) * 128, :].reshape(8, 2, 8, CHANNELS)
            for p in range(2):
                fine = rows[:, p].reshape(COLS, CHANNELS)
                old = x_ref[p, 2 * u + di].astype(jnp.float32)
                out_ref[p, 2 * u + di] = (fine + old).astype(jnp.bfloat16)


def back(blocks, cells, x, we, before):
    step = blocks[1] - blocks[0]
    fine = pl.BlockSpec((2, 16, COLS, CHANNELS), lambda i: (0, blocks[0] + step * i, 0, 0))
    specs = [
        pl.BlockSpec((64, 8, LATENT), lambda i: (i, 0, 0)),
        fine,
        pl.BlockSpec((LATENT, LATENT), lambda i: (0, 0), pipeline_mode=pl.Buffered(1)),
    ]
    args = (cells, x, we)
    aliases = {}
    if before is not None:
        specs.append(pl.BlockSpec(memory_space=pl.ANY))
        args += (before,)
        aliases = {3: 0}
    return pl.pallas_call(
        back_kernel,
        out_shape=jax.ShapeDtypeStruct((2, 64, COLS, CHANNELS), jnp.bfloat16),
        grid=(2,),
        in_specs=specs,
        out_specs=fine,
        scratch_shapes=[pltpu.VMEM((1024, CHANNELS), jnp.float32)] * 2,
        input_output_aliases=aliases,
        compiler_params=pltpu.CompilerParams(vmem_limit_bytes=20 * MIB),
        cost_estimate=pl.CostEstimate(
            flops=540_000_000, transcendentals=0, bytes_accessed=4_000_000
        ),
        name="back_inner" if blocks == INNER else "back_outer",
    )(*args)


def paired(kernel):
    none = ((0, 0), (0, 0), (0, 0))
    return jnp.concatenate(
        [
            jnp.pad(kernel, (none[0], (0, 1), none[1], none[2])),
            jnp.pad(kernel, (none[0], (1, 0), none[1], none[2])),
        ],
        axis=-1,
    ).reshape(1536, 256)


def from_before(cells, axis):
    ends = lax.axis_size(axis) - 1
    return lax.ppermute(cells, axis, [(i, i + 1) for i in range(ends)])


def from_after(cells, axis):
    ends = lax.axis_size(axis) - 1
    return lax.ppermute(cells, axis, [(i + 1, i) for i in range(ends)])


def per_device(
    x,
    conv_one,
    conv_two,
    merge_weight,
    norm_gains,
    attention_in,
    attention_out,
    dense_in,
    dense_out,
    expand_weight,
):
    lat, lon = lax.axis_index("lat"), lax.axis_index("lon")
    keep = jnp.stack(
        [lon > 0, lon < lax.axis_size("lon") - 1, lat > 0, lat < lax.axis_size("lat") - 1]
    ).astype(jnp.float32)
    left = from_before(x[:, COLS - 2 :, :].transpose(1, 0, 2), "lon")
    right = from_after(x[:, :2, :].transpose(1, 0, 2), "lon")
    w1, w2 = paired(conv_one), paired(conv_two)
    win = attention_in.T
    scale = HEAD_WIDTH**-0.5 * math.log2(math.e)
    qgain = jnp.broadcast_to(
        (norm_gains[1] * norm_gains[2] * scale)[:, None], (LATENT, 128)
    )

    def wide(rows):
        return jnp.concatenate(
            [
                jnp.zeros((2, LEAD - 2, CHANNELS), jnp.bfloat16),
                left[:, rows].transpose(1, 0, 2),
                x[rows],
                right[:, rows].transpose(1, 0, 2),
                jnp.zeros((2, STRIDE - LEAD - COLS - 2, CHANNELS), jnp.bfloat16),
            ],
            axis=1,
        )

    top = from_before(wide(slice(ROWS - 2, ROWS)), "lat")
    bottom = from_after(wide(slice(0, 2)), "lat")
    exchange = functools.partial(
        lax.all_to_all, axis_name=("lat", "lon"), split_axis=0, concat_axis=0, tiled=True
    )
    inner = front(INNER, keep, x, left, right, (), w1, w2, merge_weight)
    inner = exchange(inner)
    outer = front(OUTER, keep, x, left, right, (top, bottom), w1, w2, merge_weight)
    outer = exchange(outer)
    weights = (norm_gains, qgain, win, attention_out, dense_in, dense_out)
    inner = exchange(middle(inner, *weights))
    outer = exchange(middle(outer, *weights))
    field = x.reshape(2, 64, COLS, CHANNELS)
    result = back(INNER, inner, field, expand_weight, None)
    result = back(OUTER, outer, field, expand_weight, result)
    return result.reshape(ROWS, COLS, CHANNELS)


def solution(mesh):
    return jax.shard_map(
        per_device,
        mesh=mesh,
        in_specs=(P("lat", "lon", None), P(), P(), P(), P(), P(), P(), P(), P(), P()),
        out_specs=P("lat", "lon", None),
        check_vma=False,
    )
```

```python
import functools
import math

import jax
import jax.numpy as jnp
from jax import lax
from jax.experimental import pallas as pl
from jax.experimental.pallas import tpu as pltpu
from jax.sharding import PartitionSpec as P

CHANNELS = 128
LATENT = 512
NUM_HEADS = 16
HEAD_WIDTH = 32
MLP_WIDTH = 2048
EPSILON = 1e-06
FLOOR = 0.75
GELU_ONE = math.sqrt(2.0 / math.pi)
GELU_TWO = GELU_ONE * 0.044715

ROWS, COLS = 128, 64
PAIRS = COLS // 2
STRIDE = 80
LEAD = 8
STAGE_ROWS = 28
FIRST_ROWS = 24
FIRST_STRIDE = 40
INNER, OUTER = (1, 2), (0, 3)
WINDOWS = 4
MLP_ROWS = 512
MLP_PART = 256
GROUP = 4
CONV_ONE, CONV_TWO, MERGE = 9, 8, 8
LIMIT = 60 << 20


def gelu(v):
    half = 0.5 * v
    return half + half * jnp.tanh(v * (GELU_ONE + GELU_TWO * (v * v)))


def pair_columns(kernel_ref, out_ref):
    for dy in range(3):
        for k in range(4):
            for m in range(2):
                inside = 0 <= k - m <= 2
                if inside == (kernel_ref is None):
                    continue
                rows = slice((4 * dy + k) * CHANNELS, (4 * dy + k + 1) * CHANNELS)
                lanes = slice(m * CHANNELS, (m + 1) * CHANNELS)
                if inside:
                    out_ref[rows, lanes] = kernel_ref[dy, k - m]
                else:
                    out_ref[rows, lanes] = jnp.zeros((CHANNELS, CHANNELS), jnp.bfloat16)


def front_kernel(blocks, edge_ref, x_hbm, left_ref, right_ref, *rest):
    top_ref = bottom_ref = None
    if blocks == OUTER:
        top_ref, bottom_ref = rest[:2]
        rest = rest[2:]
    weights_hbm, out_hbm = rest[:3], rest[3]
    stage, sides, xab, firsts, fab, seconds, out_ref, x_ref = rest[4:12]
    c1_ref, c2_ref, w1_ref, w2_ref, wm_ref, sems = rest[12:]
    lat, lon = edge_ref[0], edge_ref[1]
    keep = [
        jnp.where(inside, 1.0, 0.0)
        for inside in (lon > 0, lon < edge_ref[3] - 1, lat > 0, lat < edge_ref[2] - 1)
    ]
    spans = [
        [
            (max(start, 0), min(start + 20, ROWS), max(-start, 0))
            for start in (64 * p + 16 * block - 2 for p in range(2))
        ]
        for block in blocks
    ]
    fills = [
        [
            pltpu.make_async_copy(
                x_hbm.at[pl.ds(low, high - low)],
                x_ref.at[2 * at + p, pl.ds(0, high - low)],
                sems.at[2 + 2 * at + p],
            )
            for p, (low, high, _) in enumerate(pair)
        ]
        for at, pair in enumerate(spans)
    ]
    loads = [
        pltpu.make_async_copy(source, target, sems.at[6 + i])
        for i, (source, target) in enumerate(zip(weights_hbm, (c1_ref, c2_ref, wm_ref)))
    ]
    for copy in fills[0] + loads[:1] + fills[1] + loads[1:]:
        copy.start()
    stores = [
        pltpu.make_async_copy(
            out_ref.at[pl.ds(8 * i, 8)], out_hbm.at[pl.ds(8 * i, 8)], sems.at[i]
        )
        for i in range(2)
    ]
    pair_columns(None, w1_ref)
    pair_columns(None, w2_ref)
    sides[0:2] = left_ref[...].astype(jnp.float32)
    sides[2:4] = right_ref[...].astype(jnp.float32)
    sub = lax.broadcasted_iota(jnp.int32, (4 * MERGE, 8, LATENT), 1)
    for at, block in enumerate(blocks):
        for p in range(2):
            low, high, skip = spans[at][p]
            count = high - low
            fills[at][p].wait()

            def place(r, carry, at=at, p=p, skip=skip):
                to = pl.multiple_of((p * STAGE_ROWS + skip + r) * STRIDE + LEAD, 8)
                stage[pl.ds(to, COLS), :] = x_ref[2 * at + p, r].astype(jnp.float32)
                return carry

            lax.fori_loop(0, count, place, 0, unroll=2)
            base = (p * STAGE_ROWS + skip) * STRIDE
            for c in range(2):
                stage[pl.ds(base + LEAD - 2 + c, count, stride=STRIDE), :] = sides[c, low:high, :]
                stage[pl.ds(base + LEAD + COLS + c, count, stride=STRIDE), :] = sides[
                    2 + c, low:high, :
                ]
            for ends_ref, wanted, first in (
                (top_ref, skip > 0, 0),
                (bottom_ref, skip + count < 20, 18),
            ):
                if wanted:
                    tail = ends_ref[2 * COLS :, :].astype(jnp.float32)
                    for r in range(2):
                        to = (p * STAGE_ROWS + first + r) * STRIDE + LEAD
                        stage[to : to + COLS, :] = ends_ref[r * COLS : (r + 1) * COLS].astype(
                            jnp.float32
                        )
                        for c in range(2):
                            stage[to - 2 + c : to - 1 + c, :] = tail[2 * c + r : 2 * c + r + 1]
                            stage[to + COLS + c : to + COLS + c + 1, :] = tail[
                                4 + 2 * c + r : 5 + 2 * c + r
                            ]
        for p in range(2):
            for r in range(20):
                base = (p * STAGE_ROWS + r) * STRIDE + LEAD
                xab[p, r] = jnp.concatenate(
                    [stage[pl.ds(base + k, PAIRS, stride=2), :] for k in (-2, -1, 0, 1)], axis=-1
                ).astype(jnp.bfloat16)
        if at == 0:
            loads[0].wait()
            pair_columns(c1_ref, w1_ref)
        for p in range(2):
            for r0 in range(0, 18, CONV_ONE):
                lhs = jnp.concatenate([xab[p, r0 + dy : r0 + dy + CONV_ONE] for dy in range(3)], axis=-1)
                y = gelu(
                    jnp.dot(
                        lhs.reshape(CONV_ONE * PAIRS, 1536),
                        w1_ref[...],
                        preferred_element_type=jnp.float32,
                    )
                )
                for r in range(CONV_ONE):
                    to = (p * FIRST_ROWS + r0 + r) * FIRST_STRIDE
                    for m in range(2):
                        firsts[m, to : to + PAIRS, :] = y[
                            r * PAIRS : (r + 1) * PAIRS, m * CHANNELS : (m + 1) * CHANNELS
                        ]
        lhs = jnp.concatenate(
            [
                jnp.concatenate(
                    [
                        stage[
                            pl.ds(
                                (p * STAGE_ROWS + dy) * STRIDE + LEAD + COLS - 2 + k,
                                FIRST_ROWS,
                                stride=STRIDE,
                            ),
                            :,
                        ]
                        for dy in range(3)
                        for k in range(4)
                    ],
                    axis=-1,
                )
                for p in range(2)
            ],
            axis=0,
        ).astype(jnp.bfloat16)
        edge = gelu(jnp.dot(lhs, w1_ref[...], preferred_element_type=jnp.float32))
        for p in range(2):
            base = p * FIRST_ROWS * FIRST_STRIDE
            mine = edge[p * FIRST_ROWS : (p + 1) * FIRST_ROWS]
            last = pl.ds(base + PAIRS, FIRST_ROWS, stride=FIRST_STRIDE)
            firsts[0, last, :] = mine[:, 0:CHANNELS]
            firsts[1, last, :] = mine[:, CHANNELS:] * keep[1]
            begin = pl.ds(base, FIRST_ROWS, stride=FIRST_STRIDE)
            firsts[0, begin, :] = firsts[0, begin, :] * keep[0]
        if block == 0:
            firsts[:, 0:FIRST_STRIDE, :] = firsts[:, 0:FIRST_STRIDE, :] * keep[2]
        if block == 3:
            to = (FIRST_ROWS + 17) * FIRST_STRIDE
            firsts[:, to : to + FIRST_STRIDE, :] = firsts[:, to : to + FIRST_STRIDE, :] * keep[3]
        for p in range(2):
            for r in range(18):
                base = (p * FIRST_ROWS + r) * FIRST_STRIDE
                fab[p, r] = jnp.concatenate(
                    [firsts[m, base + k : base + k + PAIRS, :] for k in range(2) for m in range(2)],
                    axis=-1,
                ).astype(jnp.bfloat16)
        if at == 0:
            loads[1].wait()
            loads[2].wait()
            pair_columns(c2_ref, w2_ref)
        for p in range(2):
            for r0 in range(0, 16, CONV_TWO):
                lhs = jnp.concatenate(
                    [fab[p, r0 + dy : r0 + dy + CONV_TWO] for dy in range(3)], axis=-1
                )
                s = gelu(
                    jnp.dot(
                        lhs.reshape(CONV_TWO * PAIRS, 1536),
                        w2_ref[...],
                        preferred_element_type=jnp.float32,
                    )
                ).astype(jnp.bfloat16)
                s = s.reshape(CONV_TWO // 2, 2, PAIRS, 256)
                to = slice(r0 // 2, (r0 + CONV_TWO) // 2)
                seconds[p, to, :, 0:256] = s[:, 0]
                seconds[p, to, :, 256:512] = s[:, 1]
        for r0 in range(0, 8, MERGE):
            zero, one = [
                jnp.dot(
                    seconds[p, r0 : r0 + MERGE].reshape(MERGE * PAIRS, LATENT),
                    wm_ref[...],
                    preferred_element_type=jnp.float32,
                ).reshape(MERGE * 4, 8, LATENT)
                for p in range(2)
            ]
            even = jnp.where(sub < 4, zero, pltpu.roll(one, 4, 1))
            odd = jnp.where(sub < 4, pltpu.roll(zero, 4, 1), one)
            to = slice(8 * at + r0, 8 * at + r0 + MERGE)
            out_ref[to, :, 0] = even.reshape(MERGE, 4, 8, LATENT).astype(jnp.bfloat16)
            out_ref[to, :, 1] = odd.reshape(MERGE, 4, 8, LATENT).astype(jnp.bfloat16)
        stores[at].start()
    for store in stores:
        store.wait()


def front(blocks, place, x, left, right, ends, c1, c2, wm):
    vmem = pl.BlockSpec(memory_space=pltpu.VMEM)
    hbm = pl.BlockSpec(memory_space=pltpu.HBM)
    args = (x, left, right) + tuple(ends) + (c1, c2, wm)
    out = pl.pallas_call(
        functools.partial(front_kernel, blocks),
        out_shape=jax.ShapeDtypeStruct((16, 4, 2, 8, LATENT), jnp.bfloat16),
        in_specs=[pl.BlockSpec(memory_space=pltpu.SMEM), hbm]
        + [vmem] * (2 + len(ends))
        + [hbm] * 3,
        out_specs=hbm,
        scratch_shapes=[
            pltpu.VMEM((2 * STAGE_ROWS * STRIDE, CHANNELS), jnp.float32),
            pltpu.VMEM((4, ROWS, CHANNELS), jnp.float32),
            pltpu.VMEM((2, 20, PAIRS, 512), jnp.bfloat16),
            pltpu.VMEM((2, 2 * FIRST_ROWS * FIRST_STRIDE, CHANNELS), jnp.float32),
            pltpu.VMEM((2, 18, PAIRS, 512), jnp.bfloat16),
            pltpu.VMEM((2, 8, PAIRS, LATENT), jnp.bfloat16),
            pltpu.VMEM((16, 4, 2, 8, LATENT), jnp.bfloat16),
            pltpu.VMEM((4, 20, COLS, CHANNELS), jnp.bfloat16),
            pltpu.VMEM((3, 3, CHANNELS, CHANNELS), jnp.bfloat16),
            pltpu.VMEM((3, 3, CHANNELS, CHANNELS), jnp.bfloat16),
            pltpu.VMEM((1536, 256), jnp.bfloat16),
            pltpu.VMEM((1536, 256), jnp.bfloat16),
            pltpu.VMEM((LATENT, LATENT), jnp.bfloat16),
            pltpu.SemaphoreType.DMA((9,)),
        ],
        compiler_params=pltpu.CompilerParams(vmem_limit_bytes=LIMIT),
        cost_estimate=pl.CostEstimate(
            flops=8_000_000_000, transcendentals=1_100_000, bytes_accessed=5_000_000
        ),
        name="front_inner" if blocks == INNER else "front_outer",
    )(place, *args)
    return out.reshape(128, 8, LATENT)


def layer_norm(v, gain):
    center = v - jnp.mean(v, axis=-1, keepdims=True)
    spread = jnp.mean(center * center, axis=-1, keepdims=True)
    return center * lax.rsqrt(spread + EPSILON) * gain


def middle_kernel(
    tok_hbm,
    gains_ref,
    qgain_ref,
    win_hbm,
    wout_hbm,
    wi_hbm,
    wd_hbm,
    out_hbm,
    cells,
    staged,
    win_ref,
    wout_ref,
    wi_ref,
    wd_ref,
    sems,
):
    sources = (wout_hbm, wi_hbm, wd_hbm)
    targets = (wout_ref, wi_ref, wd_ref)
    loads = [
        pltpu.make_async_copy(source, target, sems.at[i])
        for i, (source, target) in enumerate(zip(sources, targets))
    ]
    fills = [
        pltpu.make_async_copy(
            tok_hbm.at[pl.ds(32 * i, 32)], staged.at[pl.ds(32 * i, 32)], sems.at[3 + i]
        )
        for i in range(4)
    ]
    parts = [
        pltpu.make_async_copy(
            win_hbm.at[pl.ds(LATENT * i, LATENT)], win_ref.at[pl.ds(LATENT * i, LATENT)], sems.at[7 + i]
        )
        for i in range(3)
    ]
    for load in fills + parts + loads:
        load.start()
    for i, fill in enumerate(fills):
        fill.wait()
        held = staged[32 * i : 32 * (i + 1)].reshape(256, LATENT).astype(jnp.float32)
        for q in range(4):
            cells[q, 256 * i : 256 * (i + 1)] = held[:, q * 128 : (q + 1) * 128]
    for part in parts:
        part.wait()

    def window(step, carry):
        places = [pl.ds(step + WINDOWS * p, 128, stride=8) for p in range(2)]
        tokens = jnp.concatenate(
            [jnp.concatenate([cells[q, place, :] for q in range(4)], axis=-1) for place in places],
            axis=0,
        )
        normed = layer_norm(tokens, gains_ref[0:1, :]).astype(jnp.bfloat16)
        projected = lax.dot_general(
            win_ref[...], normed, (((1,), (1,)), ((), ())), preferred_element_type=jnp.float32
        )

        def scaled(part):
            heads = part.reshape(NUM_HEADS, HEAD_WIDTH, 256)
            square = jnp.mean(heads * heads, axis=1, keepdims=True)
            return (heads * lax.rsqrt(jnp.maximum(square, FLOOR))).reshape(LATENT, 256)

        qgain = jnp.concatenate([qgain_ref[...], qgain_ref[...]], axis=-1)
        queries = (scaled(projected[0:LATENT]) * qgain).astype(jnp.bfloat16)
        keys = scaled(projected[LATENT : 2 * LATENT]).T.astype(jnp.bfloat16)
        values = projected[2 * LATENT :].astype(jnp.bfloat16)
        blank = jnp.zeros((HEAD_WIDTH, 256), jnp.bfloat16)
        row = lax.broadcasted_iota(jnp.int32, (16, 256), 0)
        marks = [jnp.where(row == i, 1.0, 0.0).astype(jnp.bfloat16) for i in range(GROUP)]
        attended = []
        for group in range(NUM_HEADS // GROUP):
            heads = [
                slice((GROUP * group + i) * HEAD_WIDTH, (GROUP * group + i + 1) * HEAD_WIDTH)
                for i in range(GROUP)
            ]
            right = jnp.concatenate(
                [
                    jnp.concatenate([queries[heads[i]] if k == i else blank for k in range(GROUP)], axis=0)
                    for i in range(GROUP)
                ],
                axis=1,
            )
            scores = jnp.dot(
                keys[:, group * GROUP * 32 : (group + 1) * GROUP * 32], right, preferred_element_type=jnp.float32
            )
            expon = jnp.exp2(scores).astype(jnp.bfloat16)
            left = jnp.concatenate(
                [
                    jnp.concatenate(
                        [values[heads[i]] if k == i else blank for k in range(GROUP)] + [marks[i]],
                        axis=0,
                    )
                    for i in range(GROUP)
                ],
                axis=1,
            )
            stacked = jnp.concatenate([expon[:, 256 * i : 256 * (i + 1)] for i in range(GROUP)], axis=0)
            both = jnp.dot(left, stacked, preferred_element_type=jnp.float32)
            inverse = 1.0 / both[32 * GROUP : 32 * GROUP + 8]
            for i in range(GROUP):
                attended.append(both[32 * i : 32 * (i + 1)] * inverse[i : i + 1])
        attended = jnp.concatenate(attended, axis=0).T.astype(jnp.bfloat16)

        @pl.when(step == 0)
        def _():
            loads[0].wait()

        mixed = tokens + jnp.dot(attended, wout_ref[...], preferred_element_type=jnp.float32)
        for p in range(2):
            for q in range(4):
                cells[q, places[p], :] = mixed[128 * p : 128 * (p + 1), 128 * q : 128 * (q + 1)]
        return carry

    lax.fori_loop(0, WINDOWS, window, 0, unroll=2)
    loads[1].wait()
    loads[2].wait()
    stores = []
    for at in range(1024 // MLP_ROWS):
        place = slice(at * MLP_ROWS, (at + 1) * MLP_ROWS)
        mixed = jnp.concatenate([cells[q, place, :] for q in range(4)], axis=-1)
        mixed = mixed.astype(jnp.bfloat16).astype(jnp.float32)
        normed_two = layer_norm(mixed, gains_ref[3:4, :]).astype(jnp.bfloat16)
        updated = mixed
        for j in range(MLP_WIDTH // MLP_PART):
            part = slice(j * MLP_PART, (j + 1) * MLP_PART)
            inner = gelu(
                jnp.dot(normed_two, wi_ref[:, part], preferred_element_type=jnp.float32)
            ).astype(jnp.bfloat16)
            updated = updated + jnp.dot(inner, wd_ref[part, :], preferred_element_type=jnp.float32)
        blocks = pl.ds(at * (MLP_ROWS // 8), MLP_ROWS // 8)
        staged[blocks] = updated.astype(jnp.bfloat16).reshape(MLP_ROWS // 8, 8, LATENT)
        store = pltpu.make_async_copy(staged.at[blocks], out_hbm.at[blocks], sems.at[10 + at])
        store.start()
        stores.append(store)
    for store in stores:
        store.wait()


def middle(tokens, gains, qgain, win, wout, wi, wd):
    vmem = pl.BlockSpec(memory_space=pltpu.VMEM)
    hbm = pl.BlockSpec(memory_space=pltpu.HBM)
    return pl.pallas_call(
        middle_kernel,
        out_shape=jax.ShapeDtypeStruct((128, 8, LATENT), jnp.bfloat16),
        in_specs=[hbm] + [vmem] * 2 + [hbm] * 4,
        out_specs=hbm,
        scratch_shapes=[
            pltpu.VMEM((4, 1024, 128), jnp.float32),
            pltpu.VMEM((128, 8, LATENT), jnp.bfloat16),
            pltpu.VMEM((3 * LATENT, LATENT), jnp.bfloat16),
            pltpu.VMEM((LATENT, LATENT), jnp.bfloat16),
            pltpu.VMEM((LATENT, MLP_WIDTH), jnp.bfloat16),
            pltpu.VMEM((MLP_WIDTH, LATENT), jnp.bfloat16),
            pltpu.SemaphoreType.DMA((10 + 1024 // MLP_ROWS,)),
        ],
        compiler_params=pltpu.CompilerParams(vmem_limit_bytes=LIMIT),
        cost_estimate=pl.CostEstimate(
            flops=16_000_000_000, transcendentals=6_000_000, bytes_accessed=9_000_000
        ),
        name="middle",
    )(tokens, gains, qgain, win, wout, wi, wd)


def back_kernel(cells_ref, x_ref, we_ref, *rest):
    out_ref, even, odd = rest[-3:]
    expanded = jnp.dot(
        cells_ref[...].reshape(512, LATENT), we_ref[...], preferred_element_type=jnp.float32
    )
    for di, held in enumerate((even, odd)):
        for dj in range(2):
            lanes = (2 * di + dj) * CHANNELS
            held[pl.ds(dj, 512, stride=2), :] = expanded[:, lanes : lanes + CHANNELS]
    for di, held in enumerate((even, odd)):
        for u in range(8):
            rows = held[u * 128 : (u + 1) * 128, :].reshape(8, 2, 8, CHANNELS)
            for p in range(2):
                fine = rows[:, p].reshape(COLS, CHANNELS)
                old = x_ref[p, 2 * u + di].astype(jnp.float32)
                out_ref[p, 2 * u + di] = (fine + old).astype(jnp.bfloat16)


def back(blocks, cells, x, we, before):
    step = blocks[1] - blocks[0]
    fine = pl.BlockSpec((2, 16, COLS, CHANNELS), lambda i: (0, blocks[0] + step * i, 0, 0))
    specs = [
        pl.BlockSpec((64, 8, LATENT), lambda i: (i, 0, 0)),
        fine,
        pl.BlockSpec((LATENT, LATENT), lambda i: (0, 0), pipeline_mode=pl.Buffered(1)),
    ]
    args = (cells, x, we)
    aliases = {}
    if before is not None:
        specs.append(pl.BlockSpec(memory_space=pl.ANY))
        args += (before,)
        aliases = {3: 0}
    return pl.pallas_call(
        back_kernel,
        out_shape=jax.ShapeDtypeStruct((2, 64, COLS, CHANNELS), jnp.bfloat16),
        grid=(2,),
        in_specs=specs,
        out_specs=fine,
        scratch_shapes=[pltpu.VMEM((1024, CHANNELS), jnp.float32)] * 2,
        input_output_aliases=aliases,
        compiler_params=pltpu.CompilerParams(vmem_limit_bytes=16 << 20),
        cost_estimate=pl.CostEstimate(
            flops=540_000_000, transcendentals=0, bytes_accessed=4_000_000
        ),
        name="back_inner" if blocks == INNER else "back_outer",
    )(*args)


def from_before(cells, axis):
    ends = lax.axis_size(axis) - 1
    return lax.ppermute(cells, axis, [(i, i + 1) for i in range(ends)])


def from_after(cells, axis):
    ends = lax.axis_size(axis) - 1
    return lax.ppermute(cells, axis, [(i + 1, i) for i in range(ends)])


def per_device(
    x,
    conv_one,
    conv_two,
    merge_weight,
    norm_gains,
    attention_in,
    attention_out,
    dense_in,
    dense_out,
    expand_weight,
):
    place = jnp.stack(
        [
            jnp.int32(at)
            for at in (
                lax.axis_index("lat"),
                lax.axis_index("lon"),
                lax.axis_size("lat"),
                lax.axis_size("lon"),
            )
        ]
    )
    left = from_before(x[:, COLS - 2 :, :].transpose(1, 0, 2), "lon")
    right = from_after(x[:, :2, :].transpose(1, 0, 2), "lon")
    win = attention_in.T
    scale = HEAD_WIDTH**-0.5 * math.log2(math.e)
    qgain = jnp.broadcast_to(
        (norm_gains[1] * norm_gains[2] * scale)[:, None], (LATENT, 128)
    )

    def wide(rows):
        return jnp.concatenate(
            [
                x[rows].reshape(2 * COLS, CHANNELS),
                left[:, rows].reshape(4, CHANNELS),
                right[:, rows].reshape(4, CHANNELS),
            ],
            axis=0,
        )

    top = from_before(wide(slice(ROWS - 2, ROWS)), "lat")
    bottom = from_after(wide(slice(0, 2)), "lat")
    exchange = functools.partial(
        lax.all_to_all, axis_name=("lat", "lon"), split_axis=0, concat_axis=0, tiled=True
    )
    inner = front(INNER, place, x, left, right, (), conv_one, conv_two, merge_weight)
    inner, top, bottom, win = lax.optimization_barrier((inner, top, bottom, win))
    inner = exchange(inner)
    outer = front(OUTER, place, x, left, right, (top, bottom), conv_one, conv_two, merge_weight)
    outer = exchange(outer)
    weights = (norm_gains, qgain, win, attention_out, dense_in, dense_out)
    inner = exchange(middle(inner, *weights))
    outer = exchange(middle(outer, *weights))
    field = x.reshape(2, 64, COLS, CHANNELS)
    result = back(INNER, inner, field, expand_weight, None)
    result = back(OUTER, outer, field, expand_weight, result)
    return result.reshape(ROWS, COLS, CHANNELS)


def solution(mesh):
    return jax.shard_map(
        per_device,
        mesh=mesh,
        in_specs=(P("lat", "lon", None), P(), P(), P(), P(), P(), P(), P(), P(), P()),
        out_specs=P("lat", "lon", None),
        check_vma=False,
    )
```

```python
import functools
import math

import jax
import jax.numpy as jnp
from jax import lax
from jax.experimental import pallas as pl
from jax.experimental.pallas import tpu as pltpu
from jax.sharding import PartitionSpec as P

CHANNELS = 128
LATENT = 512
NUM_HEADS = 16
HEAD_WIDTH = 32
MLP_WIDTH = 2048
EPSILON = 1e-06
FLOOR = 0.75
GELU_ONE = math.sqrt(2.0 / math.pi)
GELU_TWO = GELU_ONE * 0.044715

ROWS, COLS = 128, 64
PAIRS = COLS // 2
STRIDE = 80
LEAD = 8
STAGE_ROWS = 28
FIRST_ROWS = 24
FIRST_STRIDE = 40
INNER, OUTER = (1, 2), (0, 3)
WINDOWS = 4
MLP_ROWS = 512
MLP_PART = 256
GROUP = 4
CONV_ONE, CONV_TWO, MERGE = 9, 8, 8


def gelu(v):
    half = 0.5 * v
    return half + half * jnp.tanh(v * (GELU_ONE + GELU_TWO * (v * v)))


def pair_columns(kernel_ref, out_ref):
    for dy in range(3):
        for k in range(4):
            for m in range(2):
                inside = 0 <= k - m <= 2
                if inside == (kernel_ref is None):
                    continue
                rows = slice((4 * dy + k) * CHANNELS, (4 * dy + k + 1) * CHANNELS)
                lanes = slice(m * CHANNELS, (m + 1) * CHANNELS)
                if inside:
                    out_ref[rows, lanes] = kernel_ref[dy, k - m]
                else:
                    out_ref[rows, lanes] = jnp.zeros((CHANNELS, CHANNELS), jnp.bfloat16)


def front_kernel(blocks, edge_ref, x_hbm, left_ref, right_ref, *rest):
    top_ref = bottom_ref = None
    if blocks == OUTER:
        top_ref, bottom_ref = rest[:2]
        rest = rest[2:]
    weights_hbm, out_hbm = rest[:3], rest[3]
    stage, sides, xab, firsts, fab, seconds, out_ref, x_ref = rest[4:12]
    c1_ref, c2_ref, w1_ref, w2_ref, wm_ref, sems = rest[12:]
    lat, lon = edge_ref[0], edge_ref[1]
    keep = [
        jnp.where(inside, 1.0, 0.0)
        for inside in (lon > 0, lon < edge_ref[3] - 1, lat > 0, lat < edge_ref[2] - 1)
    ]
    spans = [
        [
            (max(start, 0), min(start + 20, ROWS), max(-start, 0))
            for start in (64 * p + 16 * block - 2 for p in range(2))
        ]
        for block in blocks
    ]
    fills = [
        [
            pltpu.make_async_copy(
                x_hbm.at[pl.ds(low, high - low)],
                x_ref.at[2 * at + p, pl.ds(0, high - low)],
                sems.at[2 + 2 * at + p],
            )
            for p, (low, high, _) in enumerate(pair)
        ]
        for at, pair in enumerate(spans)
    ]
    loads = [
        pltpu.make_async_copy(source, target, sems.at[6 + i])
        for i, (source, target) in enumerate(zip(weights_hbm, (c1_ref, c2_ref, wm_ref)))
    ]
    for copy in fills[0] + loads[:1] + fills[1] + loads[1:]:
        copy.start()
    stores = [
        pltpu.make_async_copy(
            out_ref.at[pl.ds(8 * i, 8)], out_hbm.at[pl.ds(8 * i, 8)], sems.at[i]
        )
        for i in range(2)
    ]
    pair_columns(None, w1_ref)
    pair_columns(None, w2_ref)
    sides[0:2] = left_ref[...].astype(jnp.float32)
    sides[2:4] = right_ref[...].astype(jnp.float32)
    sub = lax.broadcasted_iota(jnp.int32, (4 * MERGE, 8, LATENT), 1)
    for at, block in enumerate(blocks):
        for p in range(2):
            low, high, skip = spans[at][p]
            count = high - low
            fills[at][p].wait()

            def place(r, carry, at=at, p=p, skip=skip):
                to = pl.multiple_of((p * STAGE_ROWS + skip + r) * STRIDE + LEAD, 8)
                stage[pl.ds(to, COLS), :] = x_ref[2 * at + p, r].astype(jnp.float32)
                return carry

            lax.fori_loop(0, count, place, 0, unroll=2)
            base = (p * STAGE_ROWS + skip) * STRIDE
            for c in range(2):
                stage[pl.ds(base + LEAD - 2 + c, count, stride=STRIDE), :] = sides[c, low:high, :]
                stage[pl.ds(base + LEAD + COLS + c, count, stride=STRIDE), :] = sides[
                    2 + c, low:high, :
                ]
            for ends_ref, wanted, first in (
                (top_ref, skip > 0, 0),
                (bottom_ref, skip + count < 20, 18),
            ):
                if wanted:
                    tail = ends_ref[2 * COLS :, :].astype(jnp.float32)
                    for r in range(2):
                        to = (p * STAGE_ROWS + first + r) * STRIDE + LEAD
                        stage[to : to + COLS, :] = ends_ref[r * COLS : (r + 1) * COLS].astype(
                            jnp.float32
                        )
                        for c in range(2):
                            stage[to - 2 + c : to - 1 + c, :] = tail[2 * c + r : 2 * c + r + 1]
                            stage[to + COLS + c : to + COLS + c + 1, :] = tail[
                                4 + 2 * c + r : 5 + 2 * c + r
                            ]
        for p in range(2):
            for r in range(20):
                base = (p * STAGE_ROWS + r) * STRIDE + LEAD
                xab[p, r] = jnp.concatenate(
                    [stage[pl.ds(base + k, PAIRS, stride=2), :] for k in (-2, -1, 0, 1)], axis=-1
                ).astype(jnp.bfloat16)
        if at == 0:
            loads[0].wait()
            pair_columns(c1_ref, w1_ref)
        for p in range(2):
            for r0 in range(0, 18, CONV_ONE):
                lhs = jnp.concatenate([xab[p, r0 + dy : r0 + dy + CONV_ONE] for dy in range(3)], axis=-1)
                y = gelu(
                    jnp.dot(
                        lhs.reshape(CONV_ONE * PAIRS, 1536),
                        w1_ref[...],
                        preferred_element_type=jnp.float32,
                    )
                )
                for r in range(CONV_ONE):
                    to = (p * FIRST_ROWS + r0 + r) * FIRST_STRIDE
                    for m in range(2):
                        firsts[m, to : to + PAIRS, :] = y[
                            r * PAIRS : (r + 1) * PAIRS, m * CHANNELS : (m + 1) * CHANNELS
                        ]
        lhs = jnp.concatenate(
            [
                jnp.concatenate(
                    [
                        stage[
                            pl.ds(
                                (p * STAGE_ROWS + dy) * STRIDE + LEAD + COLS - 2 + k,
                                FIRST_ROWS,
                                stride=STRIDE,
                            ),
                            :,
                        ]
                        for dy in range(3)
                        for k in range(4)
                    ],
                    axis=-1,
                )
                for p in range(2)
            ],
            axis=0,
        ).astype(jnp.bfloat16)
        edge = gelu(jnp.dot(lhs, w1_ref[...], preferred_element_type=jnp.float32))
        for p in range(2):
            base = p * FIRST_ROWS * FIRST_STRIDE
            mine = edge[p * FIRST_ROWS : (p + 1) * FIRST_ROWS]
            last = pl.ds(base + PAIRS, FIRST_ROWS, stride=FIRST_STRIDE)
            firsts[0, last, :] = mine[:, 0:CHANNELS]
            firsts[1, last, :] = mine[:, CHANNELS:] * keep[1]
            begin = pl.ds(base, FIRST_ROWS, stride=FIRST_STRIDE)
            firsts[0, begin, :] = firsts[0, begin, :] * keep[0]
        if block == 0:
            firsts[:, 0:FIRST_STRIDE, :] = firsts[:, 0:FIRST_STRIDE, :] * keep[2]
        if block == 3:
            to = (FIRST_ROWS + 17) * FIRST_STRIDE
            firsts[:, to : to + FIRST_STRIDE, :] = firsts[:, to : to + FIRST_STRIDE, :] * keep[3]
        for p in range(2):
            for r in range(18):
                base = (p * FIRST_ROWS + r) * FIRST_STRIDE
                fab[p, r] = jnp.concatenate(
                    [firsts[m, base + k : base + k + PAIRS, :] for k in range(2) for m in range(2)],
                    axis=-1,
                ).astype(jnp.bfloat16)
        if at == 0:
            loads[1].wait()
            loads[2].wait()
            pair_columns(c2_ref, w2_ref)
        for p in range(2):
            for r0 in range(0, 16, CONV_TWO):
                lhs = jnp.concatenate(
                    [fab[p, r0 + dy : r0 + dy + CONV_TWO] for dy in range(3)], axis=-1
                )
                s = gelu(
                    jnp.dot(
                        lhs.reshape(CONV_TWO * PAIRS, 1536),
                        w2_ref[...],
                        preferred_element_type=jnp.float32,
                    )
                ).astype(jnp.bfloat16)
                s = s.reshape(CONV_TWO // 2, 2, PAIRS, 256)
                to = slice(r0 // 2, (r0 + CONV_TWO) // 2)
                seconds[p, to, :, 0:256] = s[:, 0]
                seconds[p, to, :, 256:512] = s[:, 1]
        for r0 in range(0, 8, MERGE):
            zero, one = [
                jnp.dot(
                    seconds[p, r0 : r0 + MERGE].reshape(MERGE * PAIRS, LATENT),
                    wm_ref[...],
                    preferred_element_type=jnp.float32,
                ).reshape(MERGE * 4, 8, LATENT)
                for p in range(2)
            ]
            even = jnp.where(sub < 4, zero, pltpu.roll(one, 4, 1))
            odd = jnp.where(sub < 4, pltpu.roll(zero, 4, 1), one)
            to = slice(8 * at + r0, 8 * at + r0 + MERGE)
            out_ref[to, :, 0] = even.reshape(MERGE, 4, 8, LATENT).astype(jnp.bfloat16)
            out_ref[to, :, 1] = odd.reshape(MERGE, 4, 8, LATENT).astype(jnp.bfloat16)
        stores[at].start()
    for store in stores:
        store.wait()


def front(blocks, place, x, left, right, ends, c1, c2, wm):
    vmem = pl.BlockSpec(memory_space=pltpu.VMEM)
    hbm = pl.BlockSpec(memory_space=pltpu.HBM)
    args = (held(x), left, right) + tuple(ends) + (c1, c2, wm)
    out = pl.pallas_call(
        functools.partial(front_kernel, blocks),
        out_shape=pltpu.HBM((16, 4, 2, 8, LATENT), jnp.bfloat16),
        in_specs=[pl.BlockSpec(memory_space=pltpu.SMEM), hbm]
        + [vmem] * (2 + len(ends))
        + [hbm] * 3,
        out_specs=hbm,
        scratch_shapes=[
            pltpu.VMEM((2 * STAGE_ROWS * STRIDE, CHANNELS), jnp.float32),
            pltpu.VMEM((4, ROWS, CHANNELS), jnp.float32),
            pltpu.VMEM((2, 20, PAIRS, 512), jnp.bfloat16),
            pltpu.VMEM((2, 2 * FIRST_ROWS * FIRST_STRIDE, CHANNELS), jnp.float32),
            pltpu.VMEM((2, 18, PAIRS, 512), jnp.bfloat16),
            pltpu.VMEM((2, 8, PAIRS, LATENT), jnp.bfloat16),
            pltpu.VMEM((16, 4, 2, 8, LATENT), jnp.bfloat16),
            pltpu.VMEM((4, 20, COLS, CHANNELS), jnp.bfloat16),
            pltpu.VMEM((3, 3, CHANNELS, CHANNELS), jnp.bfloat16),
            pltpu.VMEM((3, 3, CHANNELS, CHANNELS), jnp.bfloat16),
            pltpu.VMEM((1536, 256), jnp.bfloat16),
            pltpu.VMEM((1536, 256), jnp.bfloat16),
            pltpu.VMEM((LATENT, LATENT), jnp.bfloat16),
            pltpu.SemaphoreType.DMA((9,)),
        ],
        compiler_params=pltpu.CompilerParams(vmem_limit_bytes=36 << 20),
        cost_estimate=pl.CostEstimate(
            flops=8_000_000_000, transcendentals=1_100_000, bytes_accessed=5_000_000
        ),
        name="front_inner" if blocks == INNER else "front_outer",
    )(place, *args)
    return out.reshape(128, 8, LATENT)


def layer_norm(v, gain):
    center = v - jnp.mean(v, axis=-1, keepdims=True)
    spread = jnp.mean(center * center, axis=-1, keepdims=True)
    return center * lax.rsqrt(spread + EPSILON) * gain


def attend(projected, qgain_ref):
    def scaled(part):
        heads = part.reshape(NUM_HEADS, HEAD_WIDTH, 256)
        square = jnp.mean(heads * heads, axis=1, keepdims=True)
        return (heads * lax.rsqrt(jnp.maximum(square, FLOOR))).reshape(LATENT, 256)

    qgain = jnp.concatenate([qgain_ref[...], qgain_ref[...]], axis=-1)
    queries = (scaled(projected[0:LATENT]) * qgain).astype(jnp.bfloat16)
    keys = scaled(projected[LATENT : 2 * LATENT]).T.astype(jnp.bfloat16)
    values = projected[2 * LATENT :].astype(jnp.bfloat16)
    blank = jnp.zeros((HEAD_WIDTH, 256), jnp.bfloat16)
    row = lax.broadcasted_iota(jnp.int32, (16, 256), 0)
    marks = [jnp.where(row == i, 1.0, 0.0).astype(jnp.bfloat16) for i in range(GROUP)]
    attended = []
    for group in range(NUM_HEADS // GROUP):
        heads = [
            slice((GROUP * group + i) * HEAD_WIDTH, (GROUP * group + i + 1) * HEAD_WIDTH)
            for i in range(GROUP)
        ]
        right = jnp.concatenate(
            [
                jnp.concatenate([queries[heads[i]] if k == i else blank for k in range(GROUP)], axis=0)
                for i in range(GROUP)
            ],
            axis=1,
        )
        scores = jnp.dot(
            keys[:, group * GROUP * 32 : (group + 1) * GROUP * 32], right, preferred_element_type=jnp.float32
        )
        expon = jnp.exp2(scores).astype(jnp.bfloat16)
        left = jnp.concatenate(
            [
                jnp.concatenate(
                    [values[heads[i]] if k == i else blank for k in range(GROUP)] + [marks[i]],
                    axis=0,
                )
                for i in range(GROUP)
            ],
            axis=1,
        )
        stacked = jnp.concatenate([expon[:, 256 * i : 256 * (i + 1)] for i in range(GROUP)], axis=0)
        both = jnp.dot(left, stacked, preferred_element_type=jnp.float32)
        inverse = 1.0 / both[32 * GROUP : 32 * GROUP + 8]
        for i in range(GROUP):
            attended.append(both[32 * i : 32 * (i + 1)] * inverse[i : i + 1])
    return jnp.concatenate(attended, axis=0).T.astype(jnp.bfloat16)


def middle_kernel(
    tok_ref,
    gains_ref,
    qgain_ref,
    win_hbm,
    wout_hbm,
    wi_hbm,
    wd_hbm,
    out_hbm,
    cells,
    staged,
    win_ref,
    wout_ref,
    wi_ref,
    wd_ref,
    sems,
):
    sources = (wout_hbm, wi_hbm, wd_hbm)
    targets = (wout_ref, wi_ref, wd_ref)
    loads = [
        pltpu.make_async_copy(source, target, sems.at[i])
        for i, (source, target) in enumerate(zip(sources, targets))
    ]
    parts = [
        pltpu.make_async_copy(
            win_hbm.at[pl.ds(LATENT * i, LATENT)], win_ref.at[pl.ds(LATENT * i, LATENT)], sems.at[7 + i]
        )
        for i in range(3)
    ]
    for load in parts + loads:
        load.start()
    for i in range(4):
        some = tok_ref[32 * i : 32 * (i + 1)].reshape(256, LATENT).astype(jnp.float32)
        for q in range(4):
            cells[q, 256 * i : 256 * (i + 1)] = some[:, q * 128 : (q + 1) * 128]
    for part in parts:
        part.wait()

    def pair(step, carry):
        places = [pl.ds(2 * step + w + WINDOWS * p, 128, stride=8) for w in range(2) for p in range(2)]
        tokens = jnp.concatenate(
            [jnp.concatenate([cells[q, place, :] for q in range(4)], axis=-1) for place in places],
            axis=0,
        )
        normed = layer_norm(tokens, gains_ref[0:1, :]).astype(jnp.bfloat16)
        projected = lax.dot_general(
            win_ref[...], normed, (((1,), (1,)), ((), ())), preferred_element_type=jnp.float32
        )
        attended = jnp.concatenate(
            [attend(projected[:, 256 * w : 256 * (w + 1)], qgain_ref) for w in range(2)], axis=0
        )

        @pl.when(step == 0)
        def _():
            loads[0].wait()

        mixed = tokens + jnp.dot(attended, wout_ref[...], preferred_element_type=jnp.float32)
        for at, place in enumerate(places):
            for q in range(4):
                cells[q, place, :] = mixed[128 * at : 128 * (at + 1), 128 * q : 128 * (q + 1)]
        return carry

    lax.fori_loop(0, WINDOWS // 2, pair, 0)
    loads[1].wait()
    loads[2].wait()
    stores = []
    for at in range(1024 // MLP_ROWS):
        place = slice(at * MLP_ROWS, (at + 1) * MLP_ROWS)
        mixed = jnp.concatenate([cells[q, place, :] for q in range(4)], axis=-1)
        mixed = mixed.astype(jnp.bfloat16).astype(jnp.float32)
        normed_two = layer_norm(mixed, gains_ref[3:4, :]).astype(jnp.bfloat16)
        updated = mixed
        for j in range(MLP_WIDTH // MLP_PART):
            part = slice(j * MLP_PART, (j + 1) * MLP_PART)
            inner = gelu(
                jnp.dot(normed_two, wi_ref[:, part], preferred_element_type=jnp.float32)
            ).astype(jnp.bfloat16)
            updated = updated + jnp.dot(inner, wd_ref[part, :], preferred_element_type=jnp.float32)
        blocks = pl.ds(at * (MLP_ROWS // 8), MLP_ROWS // 8)
        staged[blocks] = updated.astype(jnp.bfloat16).reshape(MLP_ROWS // 8, 8, LATENT)
        store = pltpu.make_async_copy(staged.at[blocks], out_hbm.at[blocks], sems.at[10 + at])
        store.start()
        stores.append(store)
    for store in stores:
        store.wait()


def middle(tokens, gains, qgain, win, wout, wi, wd):
    vmem = pl.BlockSpec(memory_space=pltpu.VMEM)
    hbm = pl.BlockSpec(memory_space=pltpu.HBM)
    return pl.pallas_call(
        middle_kernel,
        out_shape=pltpu.HBM((128, 8, LATENT), jnp.bfloat16),
        in_specs=[vmem] * 3 + [hbm] * 4,
        out_specs=hbm,
        scratch_shapes=[
            pltpu.VMEM((4, 1024, 128), jnp.float32),
            pltpu.VMEM((128, 8, LATENT), jnp.bfloat16),
            pltpu.VMEM((3 * LATENT, LATENT), jnp.bfloat16),
            pltpu.VMEM((LATENT, LATENT), jnp.bfloat16),
            pltpu.VMEM((LATENT, MLP_WIDTH), jnp.bfloat16),
            pltpu.VMEM((MLP_WIDTH, LATENT), jnp.bfloat16),
            pltpu.SemaphoreType.DMA((10 + 1024 // MLP_ROWS,)),
        ],
        compiler_params=pltpu.CompilerParams(vmem_limit_bytes=36 << 20),
        cost_estimate=pl.CostEstimate(
            flops=16_000_000_000, transcendentals=6_000_000, bytes_accessed=9_000_000
        ),
        name="middle",
    )(tokens, gains, qgain, win, wout, wi, wd)


def back_kernel(cells_ref, x_ref, we_ref, *rest):
    out_ref, even, odd = rest[-3:]
    expanded = jnp.dot(
        cells_ref[...].reshape(512, LATENT), we_ref[...], preferred_element_type=jnp.float32
    )
    for di, held in enumerate((even, odd)):
        for dj in range(2):
            lanes = (2 * di + dj) * CHANNELS
            held[pl.ds(dj, 512, stride=2), :] = expanded[:, lanes : lanes + CHANNELS]
    for di, held in enumerate((even, odd)):
        for u in range(8):
            rows = held[u * 128 : (u + 1) * 128, :].reshape(8, 2, 8, CHANNELS)
            for p in range(2):
                fine = rows[:, p].reshape(COLS, CHANNELS)
                old = x_ref[p, 2 * u + di].astype(jnp.float32)
                out_ref[p, 2 * u + di] = (fine + old).astype(jnp.bfloat16)


def back(blocks, cells, x, we, before):
    step = blocks[1] - blocks[0]
    fine = pl.BlockSpec((2, 16, COLS, CHANNELS), lambda i: (0, blocks[0] + step * i, 0, 0))
    specs = [
        pl.BlockSpec((64, 8, LATENT), lambda i: (i, 0, 0)),
        fine,
        pl.BlockSpec((LATENT, LATENT), lambda i: (0, 0), pipeline_mode=pl.Buffered(1)),
    ]
    args = (cells, x, we)
    aliases = {}
    if before is not None:
        specs.append(pl.BlockSpec(memory_space=pl.ANY))
        args += (before,)
        aliases = {3: 0}
    return pl.pallas_call(
        back_kernel,
        out_shape=jax.ShapeDtypeStruct((2, 64, COLS, CHANNELS), jnp.bfloat16),
        grid=(2,),
        in_specs=specs,
        out_specs=fine,
        scratch_shapes=[pltpu.VMEM((1024, CHANNELS), jnp.float32)] * 2,
        input_output_aliases=aliases,
        compiler_params=pltpu.CompilerParams(vmem_limit_bytes=16 << 20),
        cost_estimate=pl.CostEstimate(
            flops=540_000_000, transcendentals=0, bytes_accessed=4_000_000
        ),
        name="back_inner" if blocks == INNER else "back_outer",
    )(*args)


def held(array):
    return pltpu.with_memory_space_constraint(array, pltpu.HBM)


def from_before(cells, axis):
    ends = lax.axis_size(axis) - 1
    return lax.ppermute(cells, axis, [(i, i + 1) for i in range(ends)])


def from_after(cells, axis):
    ends = lax.axis_size(axis) - 1
    return lax.ppermute(cells, axis, [(i + 1, i) for i in range(ends)])


def per_device(
    x,
    conv_one,
    conv_two,
    merge_weight,
    norm_gains,
    attention_in,
    attention_out,
    dense_in,
    dense_out,
    expand_weight,
):
    place = jnp.stack(
        [
            jnp.int32(at)
            for at in (
                lax.axis_index("lat"),
                lax.axis_index("lon"),
                lax.axis_size("lat"),
                lax.axis_size("lon"),
            )
        ]
    )
    left = from_before(x[:, COLS - 2 :, :].transpose(1, 0, 2), "lon")
    right = from_after(x[:, :2, :].transpose(1, 0, 2), "lon")
    win = attention_in.T
    scale = HEAD_WIDTH**-0.5 * math.log2(math.e)
    qgain = jnp.broadcast_to(
        (norm_gains[1] * norm_gains[2] * scale)[:, None], (LATENT, 128)
    )

    def wide(rows):
        return jnp.concatenate(
            [
                x[rows].reshape(2 * COLS, CHANNELS),
                left[:, rows].reshape(4, CHANNELS),
                right[:, rows].reshape(4, CHANNELS),
            ],
            axis=0,
        )

    top = from_before(wide(slice(ROWS - 2, ROWS)), "lat")
    bottom = from_after(wide(slice(0, 2)), "lat")
    exchange = functools.partial(
        lax.all_to_all, axis_name=("lat", "lon"), split_axis=0, concat_axis=0, tiled=True
    )
    kernels = tuple(held(w) for w in (conv_one, conv_two, merge_weight))
    inner = front(INNER, place, x, left, right, (), *kernels)
    inner, top, bottom, win, qgain = lax.optimization_barrier((inner, top, bottom, win, qgain))
    inner = exchange(inner)
    outer = front(OUTER, place, x, left, right, (top, bottom), *kernels)
    outer = exchange(outer)
    weights = (norm_gains, qgain) + tuple(
        held(w) for w in (win, attention_out, dense_in, dense_out)
    )
    inner = exchange(middle(inner, *weights))
    outer = exchange(middle(outer, *weights))
    field = x.reshape(2, 64, COLS, CHANNELS)
    result = back(INNER, held(inner), field, held(expand_weight), None)
    result = back(OUTER, outer, field, held(expand_weight), result)
    return result.reshape(ROWS, COLS, CHANNELS)


def solution(mesh):
    return jax.shard_map(
        per_device,
        mesh=mesh,
        in_specs=(P("lat", "lon", None), P(), P(), P(), P(), P(), P(), P(), P(), P()),
        out_specs=P("lat", "lon", None),
        check_vma=False,
    )
```

```python
import functools
import math

import jax
import jax.numpy as jnp
from jax import lax
from jax.experimental import pallas as pl
from jax.experimental.pallas import tpu as pltpu
from jax.sharding import PartitionSpec as P

CHANNELS = 128
LATENT = 512
NUM_HEADS = 16
HEAD_WIDTH = 32
MLP_WIDTH = 2048
EPSILON = 1e-06
FLOOR = 0.75
GELU_ONE = math.sqrt(2.0 / math.pi)
GELU_TWO = GELU_ONE * 0.044715

ROWS, COLS = 128, 64
PAIRS = COLS // 2
STRIDE = 80
LEAD = 8
STAGE_ROWS = 28
FIRST_ROWS = 24
FIRST_STRIDE = 40
INNER, OUTER = (1, 2), (0, 3)
WINDOWS = 4
MLP_ROWS = 512
MLP_PART = 256
GROUP = 4
CONV_ONE, CONV_TWO, MERGE = 9, 8, 8


def gelu(v):
    half = 0.5 * v
    return half + half * jnp.tanh(v * (GELU_ONE + GELU_TWO * (v * v)))


def pair_columns(kernel_ref, out_ref):
    for dy in range(3):
        for k in range(4):
            for m in range(2):
                inside = 0 <= k - m <= 2
                if inside == (kernel_ref is None):
                    continue
                rows = slice((4 * dy + k) * CHANNELS, (4 * dy + k + 1) * CHANNELS)
                lanes = slice(m * CHANNELS, (m + 1) * CHANNELS)
                if inside:
                    out_ref[rows, lanes] = kernel_ref[dy, k - m]
                else:
                    out_ref[rows, lanes] = jnp.zeros((CHANNELS, CHANNELS), jnp.bfloat16)


def front_kernel(blocks, edge_ref, x_hbm, left_ref, right_ref, *rest):
    top_ref = bottom_ref = None
    if blocks == OUTER:
        top_ref, bottom_ref = rest[:2]
        rest = rest[2:]
    weights_hbm, out_hbm = rest[:3], rest[3]
    stage, sides, xab, firsts, fab, seconds, out_ref = rest[4:11]
    x_ref, c1_ref, c2_ref, wm_ref, w1_ref, w2_ref, sems = rest[11:]
    if blocks == INNER:
        c1_ref, c2_ref = weights_hbm[:2]
    lat, lon = edge_ref[0], edge_ref[1]
    keep = [
        jnp.where(inside, 1.0, 0.0)
        for inside in (lon > 0, lon < edge_ref[3] - 1, lat > 0, lat < edge_ref[2] - 1)
    ]
    spans = [
        [
            (max(start, 0), min(start + 20, ROWS), max(-start, 0))
            for start in (64 * p + 16 * block - 2 for p in range(2))
        ]
        for block in blocks
    ]
    loads = [
        pltpu.make_async_copy(source, target, sems.at[6 + i])
        for i, (source, target) in enumerate(zip(weights_hbm, (c1_ref, c2_ref, wm_ref)))
        if source is not target
    ]
    fills = []
    if blocks == OUTER:
        fills = [
            [
                pltpu.make_async_copy(
                    x_hbm.at[pl.ds(low, high - low)],
                    x_ref.at[2 * at + p, pl.ds(0, high - low)],
                    sems.at[2 + 2 * at + p],
                )
                for p, (low, high, _) in enumerate(pair)
            ]
            for at, pair in enumerate(spans)
        ]
    for copy in sum(fills[:1], []) + loads[:1] + sum(fills[1:], []) + loads[1:]:
        copy.start()
    stores = [
        pltpu.make_async_copy(
            out_ref.at[pl.ds(8 * i, 8)], out_hbm.at[pl.ds(8 * i, 8)], sems.at[i]
        )
        for i in range(2)
    ]
    pair_columns(None, w1_ref)
    pair_columns(None, w2_ref)
    sides[0:2] = left_ref[...].astype(jnp.float32)
    sides[2:4] = right_ref[...].astype(jnp.float32)
    sub = lax.broadcasted_iota(jnp.int32, (4 * MERGE, 8, LATENT), 1)
    for at, block in enumerate(blocks):
        for p in range(2):
            low, high, skip = spans[at][p]
            count = high - low
            if blocks == OUTER:
                fills[at][p].wait()

            source = x_ref.at[2 * at + p] if blocks == OUTER else x_hbm.at[pl.ds(low, count)]

            def place(r, carry, p=p, skip=skip, source=source):
                to = pl.multiple_of((p * STAGE_ROWS + skip + r) * STRIDE + LEAD, 8)
                stage[pl.ds(to, COLS), :] = source[r].astype(jnp.float32)
                return carry

            lax.fori_loop(0, count, place, 0, unroll=2)
            base = (p * STAGE_ROWS + skip) * STRIDE
            for c in range(2):
                stage[pl.ds(base + LEAD - 2 + c, count, stride=STRIDE), :] = sides[c, low:high, :]
                stage[pl.ds(base + LEAD + COLS + c, count, stride=STRIDE), :] = sides[
                    2 + c, low:high, :
                ]
            for ends_ref, wanted, first in (
                (top_ref, skip > 0, 0),
                (bottom_ref, skip + count < 20, 18),
            ):
                if wanted:
                    tail = ends_ref[2 * COLS :, :].astype(jnp.float32)
                    for r in range(2):
                        to = (p * STAGE_ROWS + first + r) * STRIDE + LEAD
                        stage[to : to + COLS, :] = ends_ref[r * COLS : (r + 1) * COLS].astype(
                            jnp.float32
                        )
                        for c in range(2):
                            stage[to - 2 + c : to - 1 + c, :] = tail[2 * c + r : 2 * c + r + 1]
                            stage[to + COLS + c : to + COLS + c + 1, :] = tail[
                                4 + 2 * c + r : 5 + 2 * c + r
                            ]
        for p in range(2):
            for r in range(20):
                base = (p * STAGE_ROWS + r) * STRIDE + LEAD
                xab[p, r] = jnp.concatenate(
                    [stage[pl.ds(base + k, PAIRS, stride=2), :] for k in (-2, -1, 0, 1)], axis=-1
                ).astype(jnp.bfloat16)
        if at == 0:
            if blocks == OUTER:
                loads[0].wait()
            pair_columns(c1_ref, w1_ref)
        for p in range(2):
            for r0 in range(0, 18, CONV_ONE):
                lhs = jnp.concatenate([xab[p, r0 + dy : r0 + dy + CONV_ONE] for dy in range(3)], axis=-1)
                y = gelu(
                    jnp.dot(
                        lhs.reshape(CONV_ONE * PAIRS, 1536),
                        w1_ref[...],
                        preferred_element_type=jnp.float32,
                    )
                )
                for r in range(CONV_ONE):
                    to = (p * FIRST_ROWS + r0 + r) * FIRST_STRIDE
                    for m in range(2):
                        firsts[m, to : to + PAIRS, :] = y[
                            r * PAIRS : (r + 1) * PAIRS, m * CHANNELS : (m + 1) * CHANNELS
                        ]
        lhs = jnp.concatenate(
            [
                jnp.concatenate(
                    [
                        stage[
                            pl.ds(
                                (p * STAGE_ROWS + dy) * STRIDE + LEAD + COLS - 2 + k,
                                FIRST_ROWS,
                                stride=STRIDE,
                            ),
                            :,
                        ]
                        for dy in range(3)
                        for k in range(4)
                    ],
                    axis=-1,
                )
                for p in range(2)
            ],
            axis=0,
        ).astype(jnp.bfloat16)
        edge = gelu(jnp.dot(lhs, w1_ref[...], preferred_element_type=jnp.float32))
        for p in range(2):
            base = p * FIRST_ROWS * FIRST_STRIDE
            mine = edge[p * FIRST_ROWS : (p + 1) * FIRST_ROWS]
            last = pl.ds(base + PAIRS, FIRST_ROWS, stride=FIRST_STRIDE)
            firsts[0, last, :] = mine[:, 0:CHANNELS]
            firsts[1, last, :] = mine[:, CHANNELS:] * keep[1]
            begin = pl.ds(base, FIRST_ROWS, stride=FIRST_STRIDE)
            firsts[0, begin, :] = firsts[0, begin, :] * keep[0]
        if block == 0:
            firsts[:, 0:FIRST_STRIDE, :] = firsts[:, 0:FIRST_STRIDE, :] * keep[2]
        if block == 3:
            to = (FIRST_ROWS + 17) * FIRST_STRIDE
            firsts[:, to : to + FIRST_STRIDE, :] = firsts[:, to : to + FIRST_STRIDE, :] * keep[3]
        for p in range(2):
            for r in range(18):
                base = (p * FIRST_ROWS + r) * FIRST_STRIDE
                fab[p, r] = jnp.concatenate(
                    [firsts[m, base + k : base + k + PAIRS, :] for k in range(2) for m in range(2)],
                    axis=-1,
                ).astype(jnp.bfloat16)
        if at == 0:
            for load in loads[1:] if blocks == OUTER else loads:
                load.wait()
            pair_columns(c2_ref, w2_ref)
        for p in range(2):
            for r0 in range(0, 16, CONV_TWO):
                lhs = jnp.concatenate(
                    [fab[p, r0 + dy : r0 + dy + CONV_TWO] for dy in range(3)], axis=-1
                )
                s = gelu(
                    jnp.dot(
                        lhs.reshape(CONV_TWO * PAIRS, 1536),
                        w2_ref[...],
                        preferred_element_type=jnp.float32,
                    )
                ).astype(jnp.bfloat16)
                s = s.reshape(CONV_TWO // 2, 2, PAIRS, 256)
                to = slice(r0 // 2, (r0 + CONV_TWO) // 2)
                seconds[p, to, :, 0:256] = s[:, 0]
                seconds[p, to, :, 256:512] = s[:, 1]
        for r0 in range(0, 8, MERGE):
            zero, one = [
                jnp.dot(
                    seconds[p, r0 : r0 + MERGE].reshape(MERGE * PAIRS, LATENT),
                    wm_ref[...],
                    preferred_element_type=jnp.float32,
                ).reshape(MERGE * 4, 8, LATENT)
                for p in range(2)
            ]
            even = jnp.where(sub < 4, zero, pltpu.roll(one, 4, 1))
            odd = jnp.where(sub < 4, pltpu.roll(zero, 4, 1), one)
            to = slice(8 * at + r0, 8 * at + r0 + MERGE)
            out_ref[to, :, 0] = even.reshape(MERGE, 4, 8, LATENT).astype(jnp.bfloat16)
            out_ref[to, :, 1] = odd.reshape(MERGE, 4, 8, LATENT).astype(jnp.bfloat16)
        stores[at].start()
    for store in stores:
        store.wait()


def front(blocks, place, x, left, right, ends, c1, c2, wm):
    vmem = pl.BlockSpec(memory_space=pltpu.VMEM)
    hbm = pl.BlockSpec(memory_space=pltpu.HBM)
    args = (x, left, right) + tuple(ends) + (c1, c2, wm)
    far = vmem if blocks == INNER else hbm
    copies = [
        pltpu.VMEM((4 if blocks == OUTER else 1, 20, COLS, CHANNELS), jnp.bfloat16),
        pltpu.VMEM((3, 3, CHANNELS, CHANNELS), jnp.bfloat16),
        pltpu.VMEM((3, 3, CHANNELS, CHANNELS), jnp.bfloat16),
        pltpu.VMEM((LATENT, LATENT), jnp.bfloat16),
    ]
    out = pl.pallas_call(
        functools.partial(front_kernel, blocks),
        out_shape=pltpu.HBM((16, 4, 2, 8, LATENT), jnp.bfloat16),
        in_specs=[pl.BlockSpec(memory_space=pltpu.SMEM), far]
        + [vmem] * (2 + len(ends))
        + [far, far, hbm],
        out_specs=hbm,
        scratch_shapes=[
            pltpu.VMEM((2 * STAGE_ROWS * STRIDE, CHANNELS), jnp.float32),
            pltpu.VMEM((4, ROWS, CHANNELS), jnp.float32),
            pltpu.VMEM((2, 20, PAIRS, 512), jnp.bfloat16),
            pltpu.VMEM((2, 2 * FIRST_ROWS * FIRST_STRIDE, CHANNELS), jnp.float32),
            pltpu.VMEM((2, 18, PAIRS, 512), jnp.bfloat16),
            pltpu.VMEM((2, 8, PAIRS, LATENT), jnp.bfloat16),
            pltpu.VMEM((16, 4, 2, 8, LATENT), jnp.bfloat16),
        ]
        + copies
        + [
            pltpu.VMEM((1536, 256), jnp.bfloat16),
            pltpu.VMEM((1536, 256), jnp.bfloat16),
            pltpu.SemaphoreType.DMA((9,)),
        ],
        compiler_params=pltpu.CompilerParams(vmem_limit_bytes=36 << 20),
        cost_estimate=pl.CostEstimate(
            flops=8_000_000_000, transcendentals=1_100_000, bytes_accessed=5_000_000
        ),
        name="front_inner" if blocks == INNER else "front_outer",
    )(place, *args)
    return out.reshape(128, 8, LATENT)


def layer_norm(v, gain):
    center = v - jnp.mean(v, axis=-1, keepdims=True)
    spread = jnp.mean(center * center, axis=-1, keepdims=True)
    return center * lax.rsqrt(spread + EPSILON) * gain


def attend(projected, qgain_ref):
    def scaled(part):
        heads = part.reshape(NUM_HEADS, HEAD_WIDTH, 256)
        square = jnp.mean(heads * heads, axis=1, keepdims=True)
        return (heads * lax.rsqrt(jnp.maximum(square, FLOOR))).reshape(LATENT, 256)

    qgain = jnp.concatenate([qgain_ref[...], qgain_ref[...]], axis=-1)
    queries = (scaled(projected[0:LATENT]) * qgain).astype(jnp.bfloat16)
    keys = scaled(projected[LATENT : 2 * LATENT]).T.astype(jnp.bfloat16)
    values = projected[2 * LATENT :].astype(jnp.bfloat16)
    blank = jnp.zeros((HEAD_WIDTH, 256), jnp.bfloat16)
    row = lax.broadcasted_iota(jnp.int32, (16, 256), 0)
    marks = [jnp.where(row == i, 1.0, 0.0).astype(jnp.bfloat16) for i in range(GROUP)]
    attended = []
    for group in range(NUM_HEADS // GROUP):
        heads = [
            slice((GROUP * group + i) * HEAD_WIDTH, (GROUP * group + i + 1) * HEAD_WIDTH)
            for i in range(GROUP)
        ]
        right = jnp.concatenate(
            [
                jnp.concatenate([queries[heads[i]] if k == i else blank for k in range(GROUP)], axis=0)
                for i in range(GROUP)
            ],
            axis=1,
        )
        scores = jnp.dot(
            keys[:, group * GROUP * 32 : (group + 1) * GROUP * 32], right, preferred_element_type=jnp.float32
        )
        expon = jnp.exp2(scores).astype(jnp.bfloat16)
        left = jnp.concatenate(
            [
                jnp.concatenate(
                    [values[heads[i]] if k == i else blank for k in range(GROUP)] + [marks[i]],
                    axis=0,
                )
                for i in range(GROUP)
            ],
            axis=1,
        )
        stacked = jnp.concatenate([expon[:, 256 * i : 256 * (i + 1)] for i in range(GROUP)], axis=0)
        both = jnp.dot(left, stacked, preferred_element_type=jnp.float32)
        inverse = 1.0 / both[32 * GROUP : 32 * GROUP + 8]
        for i in range(GROUP):
            attended.append(both[32 * i : 32 * (i + 1)] * inverse[i : i + 1])
    return jnp.concatenate(attended, axis=0).T.astype(jnp.bfloat16)


def middle_kernel(
    tok_ref,
    gains_ref,
    qgain_ref,
    win_hbm,
    wout_hbm,
    wi_hbm,
    wd_hbm,
    out_hbm,
    cells,
    staged,
    win_ref,
    wout_ref,
    wi_ref,
    wd_ref,
    sems,
):
    sources = (wout_hbm, wi_hbm, wd_hbm)
    targets = (wout_ref, wi_ref, wd_ref)
    loads = [
        pltpu.make_async_copy(source, target, sems.at[i])
        for i, (source, target) in enumerate(zip(sources, targets))
    ]
    parts = [
        pltpu.make_async_copy(
            win_hbm.at[pl.ds(LATENT * i, LATENT)], win_ref.at[pl.ds(LATENT * i, LATENT)], sems.at[7 + i]
        )
        for i in range(3)
    ]
    for load in parts + loads:
        load.start()
    for i in range(4):
        some = tok_ref[32 * i : 32 * (i + 1)].reshape(256, LATENT).astype(jnp.float32)
        for q in range(4):
            cells[q, 256 * i : 256 * (i + 1)] = some[:, q * 128 : (q + 1) * 128]
    for part in parts:
        part.wait()

    def pair(step, carry):
        places = [pl.ds(2 * step + w + WINDOWS * p, 128, stride=8) for w in range(2) for p in range(2)]
        tokens = jnp.concatenate(
            [jnp.concatenate([cells[q, place, :] for q in range(4)], axis=-1) for place in places],
            axis=0,
        )
        normed = layer_norm(tokens, gains_ref[0:1, :]).astype(jnp.bfloat16)
        projected = lax.dot_general(
            win_ref[...], normed, (((1,), (1,)), ((), ())), preferred_element_type=jnp.float32
        )
        attended = jnp.concatenate(
            [attend(projected[:, 256 * w : 256 * (w + 1)], qgain_ref) for w in range(2)], axis=0
        )

        @pl.when(step == 0)
        def _():
            loads[0].wait()

        mixed = tokens + jnp.dot(attended, wout_ref[...], preferred_element_type=jnp.float32)
        for at, place in enumerate(places):
            for q in range(4):
                cells[q, place, :] = mixed[128 * at : 128 * (at + 1), 128 * q : 128 * (q + 1)]
        return carry

    lax.fori_loop(0, WINDOWS // 2, pair, 0)
    loads[1].wait()
    loads[2].wait()
    stores = []
    for at in range(1024 // MLP_ROWS):
        place = slice(at * MLP_ROWS, (at + 1) * MLP_ROWS)
        mixed = jnp.concatenate([cells[q, place, :] for q in range(4)], axis=-1)
        mixed = mixed.astype(jnp.bfloat16).astype(jnp.float32)
        normed_two = layer_norm(mixed, gains_ref[3:4, :]).astype(jnp.bfloat16)
        updated = mixed
        for j in range(MLP_WIDTH // MLP_PART):
            part = slice(j * MLP_PART, (j + 1) * MLP_PART)
            inner = gelu(
                jnp.dot(normed_two, wi_ref[:, part], preferred_element_type=jnp.float32)
            ).astype(jnp.bfloat16)
            updated = updated + jnp.dot(inner, wd_ref[part, :], preferred_element_type=jnp.float32)
        blocks = pl.ds(at * (MLP_ROWS // 8), MLP_ROWS // 8)
        staged[blocks] = updated.astype(jnp.bfloat16).reshape(MLP_ROWS // 8, 8, LATENT)
        store = pltpu.make_async_copy(staged.at[blocks], out_hbm.at[blocks], sems.at[10 + at])
        store.start()
        stores.append(store)
    for store in stores:
        store.wait()


def middle(tokens, gains, qgain, win, wout, wi, wd):
    vmem = pl.BlockSpec(memory_space=pltpu.VMEM)
    hbm = pl.BlockSpec(memory_space=pltpu.HBM)
    return pl.pallas_call(
        middle_kernel,
        out_shape=pltpu.HBM((128, 8, LATENT), jnp.bfloat16),
        in_specs=[vmem] * 3 + [hbm] * 4,
        out_specs=hbm,
        scratch_shapes=[
            pltpu.VMEM((4, 1024, 128), jnp.float32),
            pltpu.VMEM((128, 8, LATENT), jnp.bfloat16),
            pltpu.VMEM((3 * LATENT, LATENT), jnp.bfloat16),
            pltpu.VMEM((LATENT, LATENT), jnp.bfloat16),
            pltpu.VMEM((LATENT, MLP_WIDTH), jnp.bfloat16),
            pltpu.VMEM((MLP_WIDTH, LATENT), jnp.bfloat16),
            pltpu.SemaphoreType.DMA((10 + 1024 // MLP_ROWS,)),
        ],
        compiler_params=pltpu.CompilerParams(vmem_limit_bytes=36 << 20),
        cost_estimate=pl.CostEstimate(
            flops=16_000_000_000, transcendentals=6_000_000, bytes_accessed=9_000_000
        ),
        name="middle",
    )(tokens, gains, qgain, win, wout, wi, wd)


def back_cells(cells_ref, x_ref, we_ref, loads, out_ref, even, odd):
    cells = cells_ref[...].reshape(512, LATENT)
    for di, side in enumerate((even, odd)):
        if loads:
            loads[di].wait()
        expanded = jnp.dot(
            cells, we_ref[:, 256 * di : 256 * (di + 1)], preferred_element_type=jnp.float32
        )
        for dj in range(2):
            side[pl.ds(dj, 512, stride=2), :] = expanded[:, dj * CHANNELS : (dj + 1) * CHANNELS]
    for di, side in enumerate((even, odd)):
        for u in range(8):
            rows = side[u * 128 : (u + 1) * 128, :].reshape(8, 2, 8, CHANNELS)
            for p in range(2):
                fine = rows[:, p].reshape(COLS, CHANNELS)
                old = x_ref[p, 2 * u + di].astype(jnp.float32)
                out_ref[p, 2 * u + di] = (fine + old).astype(jnp.bfloat16)


def back_kernel(blocks, *refs):
    we_ref, out_ref, even, odd, sems = refs[-5:]
    expand = [
        pltpu.make_async_copy(refs[2].at[:, lanes], we_ref.at[:, lanes], sems.at[q])
        for q, lanes in enumerate((pl.ds(0, 256), pl.ds(256, 256)))
    ]
    for load in expand:
        load.start()
    if blocks == INNER:
        cells_ref, x_hbm, we_hbm, out_hbm, kept, x_ref = refs[:6]
        spans = [(x_hbm, INNER[0], x_ref.at[0]), (x_hbm, INNER[1], x_ref.at[1])]
        spans += [(x_hbm, OUTER[0], kept.at[0]), (x_hbm, OUTER[1], kept.at[1])]
        loads = [
            pltpu.make_async_copy(x.at[:, pl.ds(16 * block, 16)], to, sems.at[4 + i])
            for i, (x, block, to) in enumerate(spans)
        ]
        for load in loads:
            load.start()
    else:
        cells_ref, x_ref, we_hbm, _, out_hbm = refs[:5]
    stores = []
    for at, block in enumerate(blocks):
        if blocks == INNER:
            loads[at].wait()
        back_cells(
            cells_ref.at[pl.ds(64 * at, 64)],
            x_ref.at[at],
            we_ref,
            expand if at == 0 else (),
            out_ref.at[at],
            even,
            odd,
        )
        store = pltpu.make_async_copy(
            out_ref.at[at], out_hbm.at[:, pl.ds(16 * block, 16)], sems.at[2 + at]
        )
        store.start()
        stores.append(store)
    for store in stores:
        store.wait()
    if blocks == INNER:
        loads[2].wait()
        loads[3].wait()


def back(blocks, cells, *others):
    vmem = pl.BlockSpec(memory_space=pltpu.VMEM)
    hbm = pl.BlockSpec(memory_space=pltpu.HBM)
    field = pltpu.HBM((2, 64, COLS, CHANNELS), jnp.bfloat16)
    part = pltpu.VMEM((2, 2, 16, COLS, CHANNELS), jnp.bfloat16)
    first = blocks == INNER
    return pl.pallas_call(
        functools.partial(back_kernel, blocks),
        out_shape=(field, part) if first else field,
        in_specs=[vmem, hbm, hbm] if first else [vmem, vmem, hbm, hbm],
        out_specs=(hbm, vmem) if first else hbm,
        scratch_shapes=([part] if first else [])
        + [
            pltpu.VMEM((LATENT, LATENT), jnp.bfloat16),
            part,
            pltpu.VMEM((1024, CHANNELS), jnp.float32),
            pltpu.VMEM((1024, CHANNELS), jnp.float32),
            pltpu.SemaphoreType.DMA((8 if first else 4,)),
        ],
        input_output_aliases={} if first else {3: 0},
        compiler_params=pltpu.CompilerParams(vmem_limit_bytes=16 << 20),
        cost_estimate=pl.CostEstimate(
            flops=540_000_000, transcendentals=0, bytes_accessed=4_000_000
        ),
        name="back_inner" if first else "back_outer",
    )(cells, *others)


def held(array):
    return pltpu.with_memory_space_constraint(array, pltpu.HBM)


def from_before(cells, axis):
    ends = lax.axis_size(axis) - 1
    return lax.ppermute(cells, axis, [(i, i + 1) for i in range(ends)])


def from_after(cells, axis):
    ends = lax.axis_size(axis) - 1
    return lax.ppermute(cells, axis, [(i + 1, i) for i in range(ends)])


def per_device(
    x,
    conv_one,
    conv_two,
    merge_weight,
    norm_gains,
    attention_in,
    attention_out,
    dense_in,
    dense_out,
    expand_weight,
):
    place = jnp.stack(
        [
            jnp.int32(at)
            for at in (
                lax.axis_index("lat"),
                lax.axis_index("lon"),
                lax.axis_size("lat"),
                lax.axis_size("lon"),
            )
        ]
    )
    left = from_before(x[:, COLS - 2 :, :].transpose(1, 0, 2), "lon")
    right = from_after(x[:, :2, :].transpose(1, 0, 2), "lon")
    win = attention_in.T
    scale = HEAD_WIDTH**-0.5 * math.log2(math.e)
    qgain = jnp.broadcast_to(
        (norm_gains[1] * norm_gains[2] * scale)[:, None], (LATENT, 128)
    )

    def wide(rows):
        return jnp.concatenate(
            [
                x[rows].reshape(2 * COLS, CHANNELS),
                left[:, rows].reshape(4, CHANNELS),
                right[:, rows].reshape(4, CHANNELS),
            ],
            axis=0,
        )

    top = from_before(wide(slice(ROWS - 2, ROWS)), "lat")
    bottom = from_after(wide(slice(0, 2)), "lat")
    exchange = functools.partial(
        lax.all_to_all, axis_name=("lat", "lon"), split_axis=0, concat_axis=0, tiled=True
    )
    merge = held(merge_weight)
    inner = front(INNER, place, x, left, right, (), conv_one, conv_two, merge)
    inner, top, bottom, win, qgain = lax.optimization_barrier((inner, top, bottom, win, qgain))
    inner = exchange(inner)
    outer = front(
        OUTER, place, held(x), left, right, (top, bottom), held(conv_one), held(conv_two), merge
    )
    outer = exchange(outer)
    weights = (norm_gains, qgain) + tuple(
        held(w) for w in (win, attention_out, dense_in, dense_out)
    )
    inner = exchange(middle(inner, *weights))
    outer = exchange(middle(outer, *weights))
    field = held(x.reshape(2, 64, COLS, CHANNELS))
    expand = held(expand_weight)
    result, rest = back(INNER, inner, field, expand)
    result = back(OUTER, outer, rest, expand, result)
    return result.reshape(ROWS, COLS, CHANNELS)


def solution(mesh):
    return jax.shard_map(
        per_device,
        mesh=mesh,
        in_specs=(P("lat", "lon", None), P(), P(), P(), P(), P(), P(), P(), P(), P()),
        out_specs=P("lat", "lon", None),
        check_vma=False,
    )
```

```python
import functools
import math

import jax
import jax.numpy as jnp
from jax import lax
from jax.experimental import pallas as pl
from jax.experimental.pallas import tpu as pltpu
from jax.sharding import PartitionSpec as P

CHANNELS = 128
LATENT = 512
NUM_HEADS = 16
HEAD_WIDTH = 32
MLP_WIDTH = 2048
EPSILON = 1e-06
FLOOR = 0.75
GELU_ONE = math.sqrt(2.0 / math.pi)
GELU_TWO = GELU_ONE * 0.044715

ROWS, COLS = 128, 64
PAIRS = COLS // 2
STRIDE = 80
LEAD = 8
STAGE_ROWS = 28
FIRST_ROWS = 24
FIRST_STRIDE = 40
INNER, OUTER = (1, 2), (0, 3)
WINDOWS = 4
MLP_ROWS = 512
MLP_PART = 256
GROUP = 4
CONV_ONE, CONV_TWO, MERGE = 9, 8, 8


def gelu(v):
    half = 0.5 * v
    return half + half * jnp.tanh(v * (GELU_ONE + GELU_TWO * (v * v)))


def pair_columns(kernel_ref, out_ref):
    for dy in range(3):
        for k in range(4):
            for m in range(2):
                inside = 0 <= k - m <= 2
                if inside == (kernel_ref is None):
                    continue
                rows = slice((4 * dy + k) * CHANNELS, (4 * dy + k + 1) * CHANNELS)
                lanes = slice(m * CHANNELS, (m + 1) * CHANNELS)
                if inside:
                    out_ref[rows, lanes] = kernel_ref[dy, k - m]
                else:
                    out_ref[rows, lanes] = jnp.zeros((CHANNELS, CHANNELS), jnp.bfloat16)


def front_kernel(blocks, edge_ref, x_hbm, left_ref, right_ref, *rest):
    top_ref = bottom_ref = None
    if blocks == OUTER:
        top_ref, bottom_ref = rest[:2]
        rest = rest[2:]
    weights_hbm, out_hbm = rest[:3], rest[3]
    stage, sides, xab, firsts, fab, seconds, out_ref = rest[4:11]
    x_ref, c1_ref, c2_ref, wm_ref, w1_ref, w2_ref, sems = rest[11:]
    if blocks == INNER:
        c1_ref, c2_ref = weights_hbm[:2]
    lat, lon = edge_ref[0], edge_ref[1]
    keep = [
        jnp.where(inside, 1.0, 0.0)
        for inside in (lon > 0, lon < edge_ref[3] - 1, lat > 0, lat < edge_ref[2] - 1)
    ]
    spans = [
        [
            (max(start, 0), min(start + 20, ROWS), max(-start, 0))
            for start in (64 * p + 16 * block - 2 for p in range(2))
        ]
        for block in blocks
    ]
    loads = [
        pltpu.make_async_copy(source, target, sems.at[6 + i])
        for i, (source, target) in enumerate(zip(weights_hbm, (c1_ref, c2_ref, wm_ref)))
        if source is not target
    ]
    fills = []
    if blocks == OUTER:
        fills = [
            [
                pltpu.make_async_copy(
                    x_hbm.at[pl.ds(low, high - low)],
                    x_ref.at[2 * at + p, pl.ds(0, high - low)],
                    sems.at[2 + 2 * at + p],
                )
                for p, (low, high, _) in enumerate(pair)
            ]
            for at, pair in enumerate(spans)
        ]
    for copy in sum(fills[:1], []) + loads[:1] + sum(fills[1:], []) + loads[1:]:
        copy.start()
    stores = [
        pltpu.make_async_copy(
            out_ref.at[pl.ds(8 * i, 8)], out_hbm.at[pl.ds(8 * i, 8)], sems.at[i]
        )
        for i in range(2)
    ]
    pair_columns(None, w1_ref)
    pair_columns(None, w2_ref)
    sides[0:2] = left_ref[...].astype(jnp.float32)
    sides[2:4] = right_ref[...].astype(jnp.float32)
    sub = lax.broadcasted_iota(jnp.int32, (4 * MERGE, 8, LATENT), 1)
    for at, block in enumerate(blocks):
        for p in range(2):
            low, high, skip = spans[at][p]
            count = high - low
            if blocks == OUTER:
                fills[at][p].wait()

            source = x_ref.at[2 * at + p] if blocks == OUTER else x_hbm.at[pl.ds(low, count)]

            def place(r, carry, p=p, skip=skip, source=source):
                to = pl.multiple_of((p * STAGE_ROWS + skip + r) * STRIDE + LEAD, 8)
                stage[pl.ds(to, COLS), :] = source[r].astype(jnp.float32)
                return carry

            lax.fori_loop(0, count, place, 0, unroll=2)
            base = (p * STAGE_ROWS + skip) * STRIDE
            for c in range(2):
                stage[pl.ds(base + LEAD - 2 + c, count, stride=STRIDE), :] = sides[c, low:high, :]
                stage[pl.ds(base + LEAD + COLS + c, count, stride=STRIDE), :] = sides[
                    2 + c, low:high, :
                ]
            for ends_ref, wanted, first in (
                (top_ref, skip > 0, 0),
                (bottom_ref, skip + count < 20, 18),
            ):
                if wanted:
                    tail = ends_ref[2 * COLS :, :].astype(jnp.float32)
                    for r in range(2):
                        to = (p * STAGE_ROWS + first + r) * STRIDE + LEAD
                        stage[to : to + COLS, :] = ends_ref[r * COLS : (r + 1) * COLS].astype(
                            jnp.float32
                        )
                        for c in range(2):
                            stage[to - 2 + c : to - 1 + c, :] = tail[2 * c + r : 2 * c + r + 1]
                            stage[to + COLS + c : to + COLS + c + 1, :] = tail[
                                4 + 2 * c + r : 5 + 2 * c + r
                            ]
        for p in range(2):
            for r in range(20):
                base = (p * STAGE_ROWS + r) * STRIDE + LEAD
                xab[p, r] = jnp.concatenate(
                    [stage[pl.ds(base + k, PAIRS, stride=2), :] for k in (-2, -1, 0, 1)], axis=-1
                ).astype(jnp.bfloat16)
        if at == 0:
            if blocks == OUTER:
                loads[0].wait()
            pair_columns(c1_ref, w1_ref)
        for p in range(2):
            for r0 in range(0, 18, CONV_ONE):
                lhs = jnp.concatenate([xab[p, r0 + dy : r0 + dy + CONV_ONE] for dy in range(3)], axis=-1)
                y = gelu(
                    jnp.dot(
                        lhs.reshape(CONV_ONE * PAIRS, 1536),
                        w1_ref[...],
                        preferred_element_type=jnp.float32,
                    )
                )
                for r in range(CONV_ONE):
                    to = (p * FIRST_ROWS + r0 + r) * FIRST_STRIDE
                    for m in range(2):
                        firsts[m, to : to + PAIRS, :] = y[
                            r * PAIRS : (r + 1) * PAIRS, m * CHANNELS : (m + 1) * CHANNELS
                        ]
        lhs = jnp.concatenate(
            [
                jnp.concatenate(
                    [
                        stage[
                            pl.ds(
                                (p * STAGE_ROWS + dy) * STRIDE + LEAD + COLS - 2 + k,
                                FIRST_ROWS,
                                stride=STRIDE,
                            ),
                            :,
                        ]
                        for dy in range(3)
                        for k in range(4)
                    ],
                    axis=-1,
                )
                for p in range(2)
            ],
            axis=0,
        ).astype(jnp.bfloat16)
        edge = gelu(jnp.dot(lhs, w1_ref[...], preferred_element_type=jnp.float32))
        for p in range(2):
            base = p * FIRST_ROWS * FIRST_STRIDE
            mine = edge[p * FIRST_ROWS : (p + 1) * FIRST_ROWS]
            last = pl.ds(base + PAIRS, FIRST_ROWS, stride=FIRST_STRIDE)
            firsts[0, last, :] = mine[:, 0:CHANNELS]
            firsts[1, last, :] = mine[:, CHANNELS:] * keep[1]
            begin = pl.ds(base, FIRST_ROWS, stride=FIRST_STRIDE)
            firsts[0, begin, :] = firsts[0, begin, :] * keep[0]
        if block == 0:
            firsts[:, 0:FIRST_STRIDE, :] = firsts[:, 0:FIRST_STRIDE, :] * keep[2]
        if block == 3:
            to = (FIRST_ROWS + 17) * FIRST_STRIDE
            firsts[:, to : to + FIRST_STRIDE, :] = firsts[:, to : to + FIRST_STRIDE, :] * keep[3]
        for p in range(2):
            for r in range(18):
                base = (p * FIRST_ROWS + r) * FIRST_STRIDE
                fab[p, r] = jnp.concatenate(
                    [firsts[m, base + k : base + k + PAIRS, :] for k in range(2) for m in range(2)],
                    axis=-1,
                ).astype(jnp.bfloat16)
        if at == 0:
            for load in loads[1:] if blocks == OUTER else loads:
                load.wait()
            pair_columns(c2_ref, w2_ref)
        for p in range(2):
            for r0 in range(0, 16, CONV_TWO):
                lhs = jnp.concatenate(
                    [fab[p, r0 + dy : r0 + dy + CONV_TWO] for dy in range(3)], axis=-1
                )
                s = gelu(
                    jnp.dot(
                        lhs.reshape(CONV_TWO * PAIRS, 1536),
                        w2_ref[...],
                        preferred_element_type=jnp.float32,
                    )
                ).astype(jnp.bfloat16)
                s = s.reshape(CONV_TWO // 2, 2, PAIRS, 256)
                to = slice(r0 // 2, (r0 + CONV_TWO) // 2)
                seconds[p, to, :, 0:256] = s[:, 0]
                seconds[p, to, :, 256:512] = s[:, 1]
        for r0 in range(0, 8, MERGE):
            zero, one = [
                jnp.dot(
                    seconds[p, r0 : r0 + MERGE].reshape(MERGE * PAIRS, LATENT),
                    wm_ref[...],
                    preferred_element_type=jnp.float32,
                ).reshape(MERGE * 4, 8, LATENT)
                for p in range(2)
            ]
            even = jnp.where(sub < 4, zero, pltpu.roll(one, 4, 1))
            odd = jnp.where(sub < 4, pltpu.roll(zero, 4, 1), one)
            to = slice(8 * at + r0, 8 * at + r0 + MERGE)
            out_ref[to, :, 0] = even.reshape(MERGE, 4, 8, LATENT).astype(jnp.bfloat16)
            out_ref[to, :, 1] = odd.reshape(MERGE, 4, 8, LATENT).astype(jnp.bfloat16)
        stores[at].start()
    for store in stores:
        store.wait()


def front(blocks, place, x, left, right, ends, c1, c2, wm):
    vmem = pl.BlockSpec(memory_space=pltpu.VMEM)
    hbm = pl.BlockSpec(memory_space=pltpu.HBM)
    args = (x, left, right) + tuple(ends) + (c1, c2, wm)
    far = vmem if blocks == INNER else hbm
    copies = [
        pltpu.VMEM((4 if blocks == OUTER else 1, 20, COLS, CHANNELS), jnp.bfloat16),
        pltpu.VMEM((3, 3, CHANNELS, CHANNELS), jnp.bfloat16),
        pltpu.VMEM((3, 3, CHANNELS, CHANNELS), jnp.bfloat16),
        pltpu.VMEM((LATENT, LATENT), jnp.bfloat16),
    ]
    out = pl.pallas_call(
        functools.partial(front_kernel, blocks),
        out_shape=pltpu.HBM((16, 4, 2, 8, LATENT), jnp.bfloat16),
        in_specs=[pl.BlockSpec(memory_space=pltpu.SMEM), far]
        + [vmem] * (2 + len(ends))
        + [far, far, hbm],
        out_specs=hbm,
        scratch_shapes=[
            pltpu.VMEM((2 * STAGE_ROWS * STRIDE, CHANNELS), jnp.float32),
            pltpu.VMEM((4, ROWS, CHANNELS), jnp.float32),
            pltpu.VMEM((2, 20, PAIRS, 512), jnp.bfloat16),
            pltpu.VMEM((2, 2 * FIRST_ROWS * FIRST_STRIDE, CHANNELS), jnp.float32),
            pltpu.VMEM((2, 18, PAIRS, 512), jnp.bfloat16),
            pltpu.VMEM((2, 8, PAIRS, LATENT), jnp.bfloat16),
            pltpu.VMEM((16, 4, 2, 8, LATENT), jnp.bfloat16),
        ]
        + copies
        + [
            pltpu.VMEM((1536, 256), jnp.bfloat16),
            pltpu.VMEM((1536, 256), jnp.bfloat16),
            pltpu.SemaphoreType.DMA((9,)),
        ],
        compiler_params=pltpu.CompilerParams(vmem_limit_bytes=36 << 20),
        cost_estimate=pl.CostEstimate(
            flops=8_000_000_000, transcendentals=1_100_000, bytes_accessed=5_000_000
        ),
        name="front_inner" if blocks == INNER else "front_outer",
    )(place, *args)
    return out.reshape(128, 8, LATENT)


def layer_norm(v, gain):
    center = v - jnp.mean(v, axis=-1, keepdims=True)
    spread = jnp.mean(center * center, axis=-1, keepdims=True)
    return center * lax.rsqrt(spread + EPSILON) * gain


def attend(projected, qgain_ref):
    def scaled(part):
        heads = part.reshape(NUM_HEADS, HEAD_WIDTH, 256)
        square = jnp.mean(heads * heads, axis=1, keepdims=True)
        return (heads * lax.rsqrt(jnp.maximum(square, FLOOR))).reshape(LATENT, 256)

    qgain = jnp.concatenate([qgain_ref[...], qgain_ref[...]], axis=-1)
    queries = (scaled(projected[0:LATENT]) * qgain).astype(jnp.bfloat16)
    keys = scaled(projected[LATENT : 2 * LATENT]).T.astype(jnp.bfloat16)
    values = projected[2 * LATENT :].astype(jnp.bfloat16)
    blank = jnp.zeros((HEAD_WIDTH, 256), jnp.bfloat16)
    row = lax.broadcasted_iota(jnp.int32, (16, 256), 0)
    marks = [jnp.where(row == i, 1.0, 0.0).astype(jnp.bfloat16) for i in range(GROUP)]
    attended = []
    for group in range(NUM_HEADS // GROUP):
        heads = [
            slice((GROUP * group + i) * HEAD_WIDTH, (GROUP * group + i + 1) * HEAD_WIDTH)
            for i in range(GROUP)
        ]
        right = jnp.concatenate(
            [
                jnp.concatenate([queries[heads[i]] if k == i else blank for k in range(GROUP)], axis=0)
                for i in range(GROUP)
            ],
            axis=1,
        )
        scores = jnp.dot(
            keys[:, group * GROUP * 32 : (group + 1) * GROUP * 32], right, preferred_element_type=jnp.float32
        )
        expon = jnp.exp2(scores).astype(jnp.bfloat16)
        left = jnp.concatenate(
            [
                jnp.concatenate(
                    [values[heads[i]] if k == i else blank for k in range(GROUP)] + [marks[i]],
                    axis=0,
                )
                for i in range(GROUP)
            ],
            axis=1,
        )
        stacked = jnp.concatenate([expon[:, 256 * i : 256 * (i + 1)] for i in range(GROUP)], axis=0)
        both = jnp.dot(left, stacked, preferred_element_type=jnp.float32)
        inverse = 1.0 / both[32 * GROUP : 32 * GROUP + 8]
        for i in range(GROUP):
            attended.append(both[32 * i : 32 * (i + 1)] * inverse[i : i + 1])
    return jnp.concatenate(attended, axis=0).T.astype(jnp.bfloat16)


def middle_kernel(
    tok_ref,
    gains_ref,
    qgain_ref,
    win_hbm,
    wout_hbm,
    wi_hbm,
    wd_hbm,
    out_hbm,
    cells,
    staged,
    win_ref,
    wout_ref,
    wi_ref,
    wd_ref,
    sems,
):
    sources = (wout_hbm, wi_hbm, wd_hbm)
    targets = (wout_ref, wi_ref, wd_ref)
    loads = [
        pltpu.make_async_copy(source, target, sems.at[i])
        for i, (source, target) in enumerate(zip(sources, targets))
    ]
    parts = [
        pltpu.make_async_copy(
            win_hbm.at[pl.ds(LATENT * i, LATENT)], win_ref.at[pl.ds(LATENT * i, LATENT)], sems.at[7 + i]
        )
        for i in range(3)
    ]
    for load in parts + loads:
        load.start()
    for i in range(4):
        some = tok_ref[32 * i : 32 * (i + 1)].reshape(256, LATENT).astype(jnp.float32)
        for q in range(4):
            cells[q, 256 * i : 256 * (i + 1)] = some[:, q * 128 : (q + 1) * 128]
    for part in parts:
        part.wait()

    def pair(step, carry):
        places = [pl.ds(2 * step + w + WINDOWS * p, 128, stride=8) for w in range(2) for p in range(2)]
        tokens = jnp.concatenate(
            [jnp.concatenate([cells[q, place, :] for q in range(4)], axis=-1) for place in places],
            axis=0,
        )
        normed = layer_norm(tokens, gains_ref[0:1, :]).astype(jnp.bfloat16)
        projected = lax.dot_general(
            win_ref[...], normed, (((1,), (1,)), ((), ())), preferred_element_type=jnp.float32
        )
        attended = jnp.concatenate(
            [attend(projected[:, 256 * w : 256 * (w + 1)], qgain_ref) for w in range(2)], axis=0
        )

        @pl.when(step == 0)
        def _():
            loads[0].wait()

        mixed = tokens + jnp.dot(attended, wout_ref[...], preferred_element_type=jnp.float32)
        for at, place in enumerate(places):
            for q in range(4):
                cells[q, place, :] = mixed[128 * at : 128 * (at + 1), 128 * q : 128 * (q + 1)]
        return carry

    lax.fori_loop(0, WINDOWS // 2, pair, 0)
    loads[1].wait()
    loads[2].wait()
    stores = []
    for at in range(1024 // MLP_ROWS):
        place = slice(at * MLP_ROWS, (at + 1) * MLP_ROWS)
        mixed = jnp.concatenate([cells[q, place, :] for q in range(4)], axis=-1)
        mixed = mixed.astype(jnp.bfloat16).astype(jnp.float32)
        normed_two = layer_norm(mixed, gains_ref[3:4, :]).astype(jnp.bfloat16)
        updated = mixed
        for j in range(MLP_WIDTH // MLP_PART):
            part = slice(j * MLP_PART, (j + 1) * MLP_PART)
            inner = gelu(
                jnp.dot(normed_two, wi_ref[:, part], preferred_element_type=jnp.float32)
            ).astype(jnp.bfloat16)
            updated = updated + jnp.dot(inner, wd_ref[part, :], preferred_element_type=jnp.float32)
        blocks = pl.ds(at * (MLP_ROWS // 8), MLP_ROWS // 8)
        staged[blocks] = updated.astype(jnp.bfloat16).reshape(MLP_ROWS // 8, 8, LATENT)
        store = pltpu.make_async_copy(staged.at[blocks], out_hbm.at[blocks], sems.at[10 + at])
        store.start()
        stores.append(store)
    for store in stores:
        store.wait()


def middle(tokens, gains, qgain, win, wout, wi, wd):
    vmem = pl.BlockSpec(memory_space=pltpu.VMEM)
    hbm = pl.BlockSpec(memory_space=pltpu.HBM)
    return pl.pallas_call(
        middle_kernel,
        out_shape=pltpu.HBM((128, 8, LATENT), jnp.bfloat16),
        in_specs=[vmem] * 3 + [hbm] * 4,
        out_specs=hbm,
        scratch_shapes=[
            pltpu.VMEM((4, 1024, 128), jnp.float32),
            pltpu.VMEM((128, 8, LATENT), jnp.bfloat16),
            pltpu.VMEM((3 * LATENT, LATENT), jnp.bfloat16),
            pltpu.VMEM((LATENT, LATENT), jnp.bfloat16),
            pltpu.VMEM((LATENT, MLP_WIDTH), jnp.bfloat16),
            pltpu.VMEM((MLP_WIDTH, LATENT), jnp.bfloat16),
            pltpu.SemaphoreType.DMA((10 + 1024 // MLP_ROWS,)),
        ],
        compiler_params=pltpu.CompilerParams(vmem_limit_bytes=36 << 20),
        cost_estimate=pl.CostEstimate(
            flops=16_000_000_000, transcendentals=6_000_000, bytes_accessed=9_000_000
        ),
        name="middle",
    )(tokens, gains, qgain, win, wout, wi, wd)


def back_cells(cells_ref, x_ref, fill, we_ref, loads, out_ref, even, odd):
    cells = cells_ref[...].reshape(512, LATENT)
    for di, side in enumerate((even, odd)):
        if loads:
            loads[di].wait()
        expanded = jnp.dot(
            cells, we_ref[:, 256 * di : 256 * (di + 1)], preferred_element_type=jnp.float32
        )
        for dj in range(2):
            side[pl.ds(dj, 512, stride=2), :] = expanded[:, dj * CHANNELS : (dj + 1) * CHANNELS]
    fill.wait()
    for di, side in enumerate((even, odd)):
        for u in range(8):
            rows = side[u * 128 : (u + 1) * 128, :].reshape(8, 2, 8, CHANNELS)
            for p in range(2):
                fine = rows[:, p].reshape(COLS, CHANNELS)
                old = x_ref[p, 2 * u + di].astype(jnp.float32)
                out_ref[p, 2 * u + di] = (fine + old).astype(jnp.bfloat16)


def back_kernel(blocks, *refs):
    cells_ref, x_hbm, weight = refs[:3]
    x_ref, we_ref, out_ref, even, odd, sems = refs[-6:]
    out_hbm = refs[-7]
    expand = []
    if blocks == INNER:
        expand = [
            pltpu.make_async_copy(weight.at[:, lanes], we_ref.at[:, lanes], sems.at[q])
            for q, lanes in enumerate((pl.ds(0, 256), pl.ds(256, 256)))
        ]
    else:
        we_ref = weight
    loads = [
        pltpu.make_async_copy(
            x_hbm.at[:, pl.ds(16 * block, 16)], x_ref.at[i], sems.at[4 + i]
        )
        for i, block in enumerate(blocks)
    ]
    for load in expand + loads:
        load.start()
    stores = []
    for at, block in enumerate(blocks):
        back_cells(
            cells_ref.at[pl.ds(64 * at, 64)],
            x_ref.at[at],
            loads[at],
            we_ref,
            expand if at == 0 else (),
            out_ref.at[at],
            even,
            odd,
        )
        store = pltpu.make_async_copy(
            out_ref.at[at], out_hbm.at[:, pl.ds(16 * block, 16)], sems.at[2 + at]
        )
        store.start()
        stores.append(store)
    for store in stores:
        store.wait()


def back(blocks, cells, *others):
    vmem = pl.BlockSpec(memory_space=pltpu.VMEM)
    hbm = pl.BlockSpec(memory_space=pltpu.HBM)
    field = pltpu.HBM((2, 64, COLS, CHANNELS), jnp.bfloat16)
    part = pltpu.VMEM((2, 2, 16, COLS, CHANNELS), jnp.bfloat16)
    first = blocks == INNER
    return pl.pallas_call(
        functools.partial(back_kernel, blocks),
        out_shape=field,
        in_specs=[vmem, hbm, hbm] if first else [vmem, hbm, vmem, hbm],
        out_specs=hbm,
        scratch_shapes=[
            part,
            pltpu.VMEM((LATENT, LATENT), jnp.bfloat16),
            part,
            pltpu.VMEM((1024, CHANNELS), jnp.float32),
            pltpu.VMEM((1024, CHANNELS), jnp.float32),
            pltpu.SemaphoreType.DMA((6,)),
        ],
        input_output_aliases={} if first else {3: 0},
        compiler_params=pltpu.CompilerParams(vmem_limit_bytes=16 << 20),
        cost_estimate=pl.CostEstimate(
            flops=540_000_000, transcendentals=0, bytes_accessed=4_000_000
        ),
        name="back_inner" if first else "back_outer",
    )(cells, *others)


def held(array):
    return pltpu.with_memory_space_constraint(array, pltpu.HBM)


def from_before(cells, axis):
    ends = lax.axis_size(axis) - 1
    return lax.ppermute(cells, axis, [(i, i + 1) for i in range(ends)])


def from_after(cells, axis):
    ends = lax.axis_size(axis) - 1
    return lax.ppermute(cells, axis, [(i + 1, i) for i in range(ends)])


def per_device(
    x,
    conv_one,
    conv_two,
    merge_weight,
    norm_gains,
    attention_in,
    attention_out,
    dense_in,
    dense_out,
    expand_weight,
):
    place = jnp.stack(
        [
            jnp.int32(at)
            for at in (
                lax.axis_index("lat"),
                lax.axis_index("lon"),
                lax.axis_size("lat"),
                lax.axis_size("lon"),
            )
        ]
    )
    left = from_before(x[:, COLS - 2 :, :].transpose(1, 0, 2), "lon")
    right = from_after(x[:, :2, :].transpose(1, 0, 2), "lon")
    win = attention_in.T
    scale = HEAD_WIDTH**-0.5 * math.log2(math.e)
    qgain = jnp.broadcast_to(
        (norm_gains[1] * norm_gains[2] * scale)[:, None], (LATENT, 128)
    )

    def wide(rows):
        return jnp.concatenate(
            [
                x[rows].reshape(2 * COLS, CHANNELS),
                left[:, rows].reshape(4, CHANNELS),
                right[:, rows].reshape(4, CHANNELS),
            ],
            axis=0,
        )

    top = from_before(wide(slice(ROWS - 2, ROWS)), "lat")
    bottom = from_after(wide(slice(0, 2)), "lat")
    exchange = functools.partial(
        lax.all_to_all, axis_name=("lat", "lon"), split_axis=0, concat_axis=0, tiled=True
    )
    merge = held(merge_weight)
    inner = front(INNER, place, x, left, right, (), conv_one, conv_two, merge)
    inner, top, bottom, win, qgain = lax.optimization_barrier((inner, top, bottom, win, qgain))
    inner = exchange(inner)
    outer = front(
        OUTER, place, held(x), left, right, (top, bottom), held(conv_one), held(conv_two), merge
    )
    outer = exchange(outer)
    weights = (norm_gains, qgain) + tuple(
        held(w) for w in (win, attention_out, dense_in, dense_out)
    )
    inner = exchange(middle(inner, *weights))
    outer = exchange(middle(outer, *weights))
    field = held(x.reshape(2, 64, COLS, CHANNELS))
    result = back(INNER, inner, field, held(expand_weight))
    result = back(OUTER, outer, field, expand_weight, result)
    return result.reshape(ROWS, COLS, CHANNELS)


def solution(mesh):
    return jax.shard_map(
        per_device,
        mesh=mesh,
        in_specs=(P("lat", "lon", None), P(), P(), P(), P(), P(), P(), P(), P(), P()),
        out_specs=P("lat", "lon", None),
        check_vma=False,
    )
```
